128 devices in a mesh: bond: 16 (over x, z), sector: 8 (over y, core).
Axes of the slice: x: 4, y: 4, z: 4, core: 2. Of those that a mesh axis runs over, the one named last changes fastest.
Arguments:
- theta: bfloat16 [8, 768, 768], P('sector'), may hold values from -80 to 80
- sector_dims: int32 [8], P('sector'), may hold values from 1 to 768, 4608 in all
- right_dims: int32 [8], P('sector'), may hold values from 1 to 768, 4608 in all
- env_left: bfloat16 [32, 8, 768, 768], P('bond', 'sector'), may hold values from -0.21875 to 0.21875
- env_right: bfloat16 [32, 8, 768, 768], P('bond', 'sector'), may hold values from -0.21875 to 0.21875
- mpo_on: int32 [32], P('bond'), may hold values 0 or 1
- mpo_coef: float32 [32], P('bond'), may hold values from -3 to 3
- mix_index: int32 [32, 3], P('bond'), may hold values from 0 to 7
- weight_table: float32 [8], replicated, may hold values from -3 to 3
Outputs:
- matvec: bfloat16 [8, 768, 768], P('sector', 'bond')
- env_next: bfloat16 [32, 8, 768, 768], P('bond', 'sector')
The draws below stay inside these ranges and needn't reach their ends.
All inputs are finite; a program needn't handle non-finite values. No bound on the sum of `sector_dims` or of `right_dims` or of `mpo_on` on one device may be relied on, other than what follows from the above.
Results may differ from the reference program's by a relative error of at most 0.008.
Values may be sent and summed in bfloat16 or wider, within the bound.
A program may use at most 64 MiB of HBM per device.

```python
import math
import jax
import jax.numpy as jnp
import numpy as np
from jax import lax

DS = 768
NW = 8
BOND = 32
NSEC = 8


def draw_theta(key, part):
    key_base, key_row, key_col = jax.random.split(key, 3)
    sector_pos = jnp.arange(NSEC, dtype=jnp.float32) / max(NSEC - 1, 1)
    sector_scale = jnp.sqrt(1.0 + 2.0 * sector_pos)[:, None, None]
    base = jnp.clip(jax.random.normal(key_base, (NSEC, DS, DS), jnp.float32), -4.0, 4.0)
    row_scale = jnp.exp(jax.random.uniform(key_row, (NSEC, DS, 1), jnp.float32, math.log(0.3), math.log(3.0)))
    col_scale = jnp.exp(jax.random.uniform(key_col, (NSEC, 1, DS), jnp.float32, math.log(0.3), math.log(3.0)))
    return (base * row_scale * col_scale * sector_scale).astype(jnp.bfloat16)


def touch_ends(result, key, smallest, largest):
    place = [jax.random.randint(jax.random.fold_in(key, axis), (), 0, length) for axis, length in enumerate(result.shape)]
    longest = result.shape.index(max(result.shape))
    next_to = place[:longest] + [(place[longest] + 1) % result.shape[longest]] + place[longest + 1:]
    return result.at[tuple(place)].set(smallest).at[tuple(next_to)].set(largest)


def block_scale(key, dims, pieces, low, largest):
    loudness, own = 1.0, jax.random.fold_in(key, 6)
    for axis_at, blocks in pieces:
        draws = jnp.exp(jax.random.uniform(jax.random.fold_in(own, axis_at), (blocks,), jnp.float32, low / len(pieces), largest / len(pieces)))
        loudness = loudness * jnp.repeat(draws, dims[axis_at] // blocks).reshape([-1 if axis == axis_at else 1 for axis in range(len(dims))])
    return loudness


def profile(count, total, reach, skew):
    weights = [(1 << 20) // math.isqrt(standing ** skew) + 1 for standing in range(2, count + 1)]
    surplus, given = total - reach - (count - 1), [1] * (count - 1)
    while surplus > 0:
        candidates = [i for i in range(count - 1) if given[i] < reach]
        whole, left = sum([weights[i] for i in candidates]), surplus
        for i in candidates:
            extra = min(reach - given[i], max(1, left * weights[i] // whole), surplus)
            given[i] = given[i] + extra
            surplus = surplus - extra
    return np.array([reach] + given)


def ragged(own_key, count, total, reach, lean):
    if count == 2:
        one = jax.random.randint(own_key, (), max(1, total - reach), min(reach, total - 1) + 1)
        return jnp.stack([one, total - one])
    lengths = jnp.asarray(profile(count, total, reach, lean), jnp.int32)
    pairs = (count - 1) // 2
    giver, sink = lengths[1:1 + 2 * pairs:2], lengths[2:2 + 2 * pairs:2]
    margin = jnp.minimum(giver - 1, reach - sink)
    moved = jax.random.randint(jax.random.fold_in(own_key, 1), (pairs,), 0, 1 << 20) % (margin + 1)
    lengths = lengths.at[1:1 + 2 * pairs:2].set(giver - moved).at[2:2 + 2 * pairs:2].set(sink + moved)
    return lengths[jax.random.permutation(jax.random.fold_in(own_key, 2), count)]


def bell_draw(key, extent, spread, limit, shards=(), held_as=jnp.bfloat16):
    level = block_scale(key, extent, shards, -0.22, 0.18) if shards else 1.0
    entries = jax.random.normal(key, extent, jnp.float32) * spread * level
    return jnp.minimum(jnp.maximum(entries, -limit), limit).astype(held_as)


def setup_inputs(seed: int = 0) -> dict:
    arg_keys = jax.random.split(jax.random.key(seed), 10)
    theta = draw_theta(jax.random.fold_in(arg_keys[9], 71), 0)
    sector_dims = ragged(arg_keys[1], NSEC, NSEC * DS * 3 // 4, DS, 1).astype(jnp.int32)
    right_dims = ragged(arg_keys[2], NSEC, NSEC * DS * 3 // 4, DS, 1).astype(jnp.int32)
    env_left = bell_draw(arg_keys[3], (BOND, NSEC, DS, DS), DS ** -0.5, 0.21875, ((0, 16), (1, 8)))
    env_right = bell_draw(arg_keys[4], (BOND, NSEC, DS, DS), DS ** -0.5, 0.21875, ((0, 16), (1, 8)))
    mpo_on = touch_ends((jax.random.randint(arg_keys[5], (BOND,), 0, 4) < 3).astype(jnp.int32), jax.random.fold_in(arg_keys[5], 1), 0, 1)
    mpo_coef = bell_draw(arg_keys[6], (BOND,), 0.3, 3.0, ((0, 16),), jnp.float32)
    mix_index = touch_ends(jax.random.randint(arg_keys[7], (BOND, 3), 0, NW), jax.random.fold_in(arg_keys[7], 1), 0, NW - 1).astype(jnp.int32)
    weight_table = bell_draw(arg_keys[8], (NW,), 0.6, 3.0, (), jnp.float32)
    return dict(theta=theta, sector_dims=sector_dims, right_dims=right_dims, env_left=env_left, env_right=env_right, mpo_on=mpo_on, mpo_coef=mpo_coef, mix_index=mix_index, weight_table=weight_table)


def reference(theta, sector_dims, right_dims, env_left, env_right, mpo_on, mpo_coef, mix_index, weight_table):
    index = jnp.arange(DS, dtype=jnp.int32)
    row_live = (index[None, :] < sector_dims[:, None]).astype(jnp.float32)
    col_live = (index[None, :] < right_dims[:, None]).astype(jnp.float32)
    block_mask = row_live[:, :, None] * col_live[:, None, :]
    live = (theta.astype(jnp.float32) * block_mask).astype(jnp.bfloat16)
    gain = mpo_coef * mpo_on.astype(jnp.float32)
    mix_gain = weight_table[mix_index]
    left_moved = jnp.moveaxis(env_left, 1, 0)
    right_moved = jnp.moveaxis(env_right, 1, 0)

    def sector_matvec(items):
        live_block, left_block, right_block, mask_block = items
        applied = jnp.einsum('wab,bc->wac', left_block.astype(jnp.float32), live_block.astype(jnp.float32)).astype(jnp.bfloat16)
        terms = jnp.einsum('wac,wdc->wad', applied.astype(jnp.float32), right_block.astype(jnp.float32))
        return mask_block * jnp.einsum('w,wad->ad', gain, terms)
    product_sum = lax.map(sector_matvec, (live, left_moved, right_moved, block_mask))
    matvec = product_sum.astype(jnp.bfloat16)
    square_total = jnp.sum(product_sum * product_sum)
    unit = (product_sum * lax.rsqrt(square_total / (NSEC * DS * DS) + 1e-06)).astype(jnp.bfloat16)

    def sector_grow(items):
        unit_block, left_block = items
        zero = jnp.zeros((1, DS, DS), jnp.bfloat16)
        padded = jnp.concatenate([zero, left_block, zero], axis=0).astype(jnp.float32)
        mixed = (mix_gain[:, 0, None, None] * padded[:-2] + mix_gain[:, 1, None, None] * padded[1:-1] + mix_gain[:, 2, None, None] * padded[2:]).astype(jnp.bfloat16)
        half = jnp.einsum('wab,bc->wac', mixed.astype(jnp.float32), unit_block.astype(jnp.float32)).astype(jnp.bfloat16)
        grown = jnp.einsum('ba,wbc->wac', unit_block.astype(jnp.float32), half.astype(jnp.float32))
        return (grown / math.sqrt(DS)).astype(jnp.bfloat16)
    grown_all = lax.map(sector_grow, (unit, left_moved))
    env_next = jnp.moveaxis(grown_all, 0, 1)
    return (matvec, env_next)
```

```python
import math

import jax
import jax.numpy as jnp
from jax import lax
from jax.experimental import pallas as pl
from jax.experimental.pallas import tpu as pltpu
from jax.sharding import Mesh
from jax.sharding import PartitionSpec as P

AXES = ("bond_0", "bond_1", "sector_0", "sector_1")
BOND = ("bond_0", "bond_1")
SECTOR = ("sector_0", "sector_1")
MESH = pl.DeviceIdType.MESH
F32 = jnp.float32
BF16 = jnp.bfloat16

N = 768
BLK = 48
PIECES = 6
EARLY = 4
PIECE = N // PIECES
TILE = 256

RELAY_UP, RELAY_DOWN, UP_B, DOWN_A, UP_A, DOWN_B = range(6)
RS_Z = 6
AG_Z = 9
AG_UP = 12
AG_DOWN = 16
FWD = 20
SUM_CORE = 24
SUM_Y = 25
SUM_X = 28
SUM_Z = 31
HALO_UP = 34
HALO_DOWN = HALO_UP + PIECES
COPIES = HALO_DOWN + PIECES


def body(
    theta_h, left_h, right_h, rows_s, cols_s, on_s, coef_s, index_s, table_s,
    matvec_o, env_o,
    live, left, right, low, high, acc, relay_out, relay_in, side_out, from_left, from_right,
    z_out, z_in, unit, part, part_in, mixed, half, grown,
    load_sem, send_sem, recv_sem, store_sem,
):
    x = lax.axis_index("bond_0")
    z = lax.axis_index("bond_1")
    y = lax.axis_index("sector_0")
    c = lax.axis_index("sector_1")

    def at_x(d):
        return {"bond_0": lax.rem(x + d, 4)}

    def at_z(d):
        return {"bond_1": lax.rem(z + d, 4)}

    def at_y(d):
        return {"sector_0": lax.rem(y + d, 4)}

    other = {"sector_1": 1 - c}
    bond = x * 4 + z
    above = lax.rem(bond + 1, 16)
    below = lax.rem(bond + 15, 16)
    up = {"bond_0": above // 4, "bond_1": lax.rem(above, 4)}
    down = {"bond_0": below // 4, "bond_1": lax.rem(below, 4)}
    peers = [at_x(1), at_x(2), at_x(3), at_z(1), at_z(2), at_z(3), at_y(1), at_y(2), at_y(3), other, up, down]

    def remote(i, src, dst, device):
        return pltpu.make_async_remote_copy(
            src_ref=src, dst_ref=dst, send_sem=send_sem.at[i], recv_sem=recv_sem.at[i],
            device_id=device, device_id_type=MESH,
        )

    loads = [
        pltpu.make_async_copy(theta_h.at[0], live, load_sem.at[0]),
        pltpu.make_async_copy(left_h.at[0, 0], left.at[0], load_sem.at[1]),
        pltpu.make_async_copy(left_h.at[1, 0], left.at[1], load_sem.at[2]),
        pltpu.make_async_copy(right_h.at[0, 0], right.at[0], load_sem.at[3]),
        pltpu.make_async_copy(right_h.at[1, 0], right.at[1], load_sem.at[4]),
    ]
    barrier = pltpu.get_barrier_semaphore()
    for peer in peers:
        pl.semaphore_signal(barrier, inc=1, device_id=peer, device_id_type=MESH)
    for load in loads:
        load.start()
    pl.semaphore_wait(barrier, len(peers))

    def halo_up(p):
        rows = pl.ds(p * PIECE, PIECE)
        return remote(HALO_UP + p, left_h.at[1, 0, rows], low.at[rows], up)

    def halo_down(p):
        rows = pl.ds(p * PIECE, PIECE)
        return remote(HALO_DOWN + p, left_h.at[0, 0, rows], high.at[rows], down)

    for p in range(EARLY):
        halo_up(p).start()
        halo_down(p).start()

    row_dim = rows_s[0]
    col_dim = cols_s[0]
    loads[0].wait()

    @pl.loop(0, N // 128)
    def _(i):
        rows = pl.ds(pl.multiple_of(i * 128, 128), 128)
        row_id = lax.broadcasted_iota(jnp.int32, (128, N), 0) + i * 128
        col_id = lax.broadcasted_iota(jnp.int32, (128, N), 1)
        keep = (row_id < row_dim) & (col_id < col_dim)
        live[rows] = jnp.where(keep, live[rows].astype(F32), 0.0).astype(BF16)

    for load in loads[1:]:
        load.wait()

    gains = [coef_s[w] * on_s[w].astype(F32) for w in range(2)]

    relay_up = remote(RELAY_UP, relay_out.at[0], relay_in.at[0], at_x(1))
    relay_down = remote(RELAY_DOWN, relay_out.at[1], relay_in.at[1], at_x(3))
    up_b = remote(UP_B, side_out.at[0, pl.ds(2, 2)], from_left.at[pl.ds(2, 2)], at_x(1))
    up_a = remote(UP_A, side_out.at[0, pl.ds(0, 2)], from_left.at[pl.ds(0, 2)], at_x(1))
    down_a = remote(DOWN_A, side_out.at[1, pl.ds(0, 2)], from_right.at[pl.ds(0, 2)], at_x(3))
    down_b = remote(DOWN_B, side_out.at[1, pl.ds(2, 2)], from_right.at[pl.ds(2, 2)], at_x(3))

    @pl.loop(0, 4)
    def _(i):
        owner = lax.rem(x + 2 + i, 4)
        rows = pl.ds(pl.multiple_of(owner * 192, 64), 192)
        total = None
        for w in range(2):
            applied = jnp.dot(left[w, rows, :], live[...], preferred_element_type=F32).astype(BF16)
            term = gains[w] * lax.dot_general(
                applied, right[w], (((1,), (1,)), ((), ())), preferred_element_type=F32
            )
            total = term if total is None else total + term
        acc[i] = total.reshape(4, BLK, N)

        @pl.when(i == 0)
        def _():
            relay_out[0] = acc[0, 0:2].astype(BF16)
            relay_up.start()
            relay_out[1] = acc[0, 2:4].astype(BF16)
            relay_down.start()

        @pl.when(i == 1)
        def _():
            side_out[1, 0:2] = acc[1, 0:2].astype(BF16)
            down_a.start()

        @pl.when(i == 3)
        def _():
            side_out[0, 2:4] = acc[3, 2:4].astype(BF16)
            up_b.start()

    relay_up.wait_recv()
    side_out[0, 0:2] = (acc[3, 0:2] + relay_in[0].astype(F32)).astype(BF16)
    up_a.start()
    relay_down.wait_recv()
    side_out[1, 2:4] = (acc[1, 2:4] + relay_in[1].astype(F32)).astype(BF16)
    down_b.start()

    up_b.wait_recv()
    down_a.wait_recv()
    up_a.wait_recv()
    down_b.wait_recv()

    def row_sum(j):
        return acc[2, j] + from_left[j].astype(F32) + from_right[j].astype(F32)

    rs_z = {d: remote(RS_Z + d - 1, z_out.at[d - 1], z_in.at[d - 1], at_z(d)) for d in (1, 2, 3)}
    for d in (2, 1, 3):
        z_out[d - 1] = row_sum(lax.rem(z + d, 4)).astype(BF16)
        rs_z[d].start()
    mine = row_sum(z)
    for d in (1, 3, 2):
        rs_z[d].wait_recv()
        mine = mine + z_in[d - 1].astype(F32)
    row_id = lax.broadcasted_iota(jnp.int32, (BLK, N), 0) + bond * BLK
    col_id = lax.broadcasted_iota(jnp.int32, (BLK, N), 1)
    mine = jnp.where((row_id < row_dim) & (col_id < col_dim), mine, 0.0)
    rounded = mine.astype(BF16)
    unit[bond] = rounded

    def block(cx, r):
        return unit.at[lax.rem(x + cx, 4) * 4 + lax.rem(z + 4 - r, 4)]

    ag_z = {d: remote(AG_Z + d - 1, unit.at[bond], unit.at[bond], at_z(d)) for d in (1, 2, 3)}
    for d in (2, 1, 3):
        ag_z[d].start()
    ag_up = [remote(AG_UP + r, block(0, r), block(0, r), at_x(1)) for r in range(4)]
    ag_down = [remote(AG_DOWN + r, block(0, r), block(0, r), at_x(3)) for r in range(4)]
    ag_up[0].start()
    ag_down[0].start()

    matvec_o[...] = rounded
    square = mine * mine
    tile = jnp.zeros((8, 128), F32)
    for a in range(BLK // 8):
        for b in range(N // 128):
            tile = tile + square[a * 8 : a * 8 + 8, b * 128 : b * 128 + 128]
    part[0] = tile

    def spread(i, slot, devices):
        return [
            remote(i + n, part.at[slot], part_in.at[i - SUM_CORE + n], device) for n, device in enumerate(devices)
        ]

    sums = [
        spread(SUM_CORE, 0, [other]),
        spread(SUM_Y, 1, [at_y(1), at_y(2), at_y(3)]),
        spread(SUM_X, 2, [at_x(1), at_x(2), at_x(3)]),
        spread(SUM_Z, 3, [at_z(1), at_z(2), at_z(3)]),
    ]
    firsts = [0, 1, 4, 7]

    def sum_start(stage):
        for copy in sums[stage]:
            copy.start()

    def sum_finish(stage):
        total = part[stage]
        for n, copy in enumerate(sums[stage]):
            copy.wait_recv()
            total = total + part_in[firsts[stage] + n]
        part[stage + 1] = total

    sum_start(0)
    for d in (1, 3, 2):
        remote(AG_Z + d - 1, block(0, d), block(0, d), at_z(d)).wait_recv()
        ag_up[d].start()
        ag_down[d].start()
    for p in range(EARLY, PIECES):
        halo_up(p).start()
        halo_down(p).start()
    sum_finish(0)
    sum_start(1)

    w_gain = [[table_s[index_s[w, k]] for k in range(3)] for w in range(2)]
    low_gain = jnp.where(bond > 0, w_gain[0][0], 0.0)
    high_gain = jnp.where(bond < 15, w_gain[1][2], 0.0)

    def mix(p):
        rows = pl.ds(p * PIECE, PIECE)
        halo_up(p).wait_recv()
        halo_down(p).wait_recv()
        here = left[0, rows].astype(F32)
        there = left[1, rows].astype(F32)
        mixed[0, rows] = (low_gain * low[rows].astype(F32) + w_gain[0][1] * here + w_gain[0][2] * there).astype(BF16)
        mixed[1, rows] = (w_gain[1][0] * here + w_gain[1][1] * there + high_gain * high[rows].astype(F32)).astype(BF16)

    def arrive(i, cx, r):
        remote(i + r, block(cx, r), block(cx, r), at_x(1)).wait_recv()

    fwd = {
        0: remote(FWD, block(3, 0), block(3, 0), at_x(1)),
        3: remote(FWD + 3, block(3, 3), block(3, 3), at_x(1)),
        1: remote(FWD + 1, block(1, 1), block(1, 1), at_x(3)),
        2: remote(FWD + 2, block(1, 2), block(1, 2), at_x(3)),
    }
    arrive(AG_UP, 3, 0)
    fwd[0].start()
    arrive(AG_DOWN, 1, 0)
    arrive(AG_DOWN, 1, 1)
    fwd[1].start()
    arrive(AG_UP, 3, 1)
    sum_finish(1)
    sum_start(2)
    arrive(AG_UP, 3, 3)
    fwd[3].start()
    arrive(AG_DOWN, 1, 3)
    arrive(AG_DOWN, 1, 2)
    fwd[2].start()
    arrive(AG_UP, 3, 2)
    sum_finish(2)
    sum_start(3)
    for p in range(EARLY):
        mix(p)
    sum_finish(3)
    square_total = jnp.sum(part[4])
    scale = lax.rsqrt(jnp.full((1, N), square_total * (1.0 / (8 * N * N)) + 1e-06, F32))
    for p in range(EARLY, PIECES):
        mix(p)
    for r in range(4):
        remote(FWD + r, block(2, r), block(2, r), at_x(1)).wait_recv()

    @pl.loop(0, 2)
    def _(w):
        for k in range(N // TILE):
            rows = pl.ds(k * TILE, TILE)
            product = jnp.dot(mixed[w, rows, :], unit[...].reshape(N, N), preferred_element_type=F32)
            half[rows] = (product * scale).astype(BF16)
        for k in range(N // TILE):
            rows = pl.ds(k * TILE, TILE)
            side = unit[:, :, k * TILE : (k + 1) * TILE].reshape(N, TILE)
            product = lax.dot_general(side, half[...], (((0,), (0,)), ((), ())), preferred_element_type=F32)
            grown[w, rows] = (product * (scale * (1.0 / math.sqrt(N)))).astype(BF16)
        pltpu.make_async_copy(grown.at[w], env_o.at[w, 0], store_sem.at[w]).start()

    for copy in (relay_up, relay_down, up_a, up_b, down_a, down_b):
        copy.wait_send()
    for d in (1, 2, 3):
        rs_z[d].wait_send()
        ag_z[d].wait_send()
    for r in range(4):
        ag_up[r].wait_send()
        ag_down[r].wait_send()
        fwd[r].wait_send()
    for stage in sums:
        for copy in stage:
            copy.wait_send()
    for p in range(PIECES):
        halo_up(p).wait_send()
        halo_down(p).wait_send()
    for w in range(2):
        pltpu.make_async_copy(grown.at[w], env_o.at[w, 0], store_sem.at[w]).wait()


def on_device(
    theta, sector_dims, right_dims, env_left, env_right, mpo_on, mpo_coef, mix_index, weight_table
):
    hbm = pl.BlockSpec(memory_space=pl.ANY)
    smem = pl.BlockSpec(memory_space=pltpu.SMEM)
    matvec, env_next = pl.pallas_call(
        body,
        out_shape=(
            jax.ShapeDtypeStruct((BLK, N), BF16),
            jax.ShapeDtypeStruct(env_left.shape, BF16),
        ),
        in_specs=[hbm, hbm, hbm, smem, smem, smem, smem, smem, smem],
        out_specs=(pl.BlockSpec(memory_space=pltpu.VMEM), hbm),
        scratch_shapes=[
            pltpu.VMEM((N, N), BF16),
            pltpu.VMEM((2, N, N), BF16),
            pltpu.VMEM((2, N, N), BF16),
            pltpu.VMEM((N, N), BF16),
            pltpu.VMEM((N, N), BF16),
            pltpu.VMEM((4, 4, BLK, N), F32),
            pltpu.VMEM((2, 2, BLK, N), BF16),
            pltpu.VMEM((2, 2, BLK, N), BF16),
            pltpu.VMEM((2, 4, BLK, N), BF16),
            pltpu.VMEM((4, BLK, N), BF16),
            pltpu.VMEM((4, BLK, N), BF16),
            pltpu.VMEM((3, BLK, N), BF16),
            pltpu.VMEM((3, BLK, N), BF16),
            pltpu.VMEM((16, BLK, N), BF16),
            pltpu.VMEM((5, 8, 128), F32),
            pltpu.VMEM((10, 8, 128), F32),
            pltpu.VMEM((2, N, N), BF16),
            pltpu.VMEM((N, N), BF16),
            pltpu.VMEM((2, N, N), BF16),
            pltpu.SemaphoreType.DMA((5,)),
            pltpu.SemaphoreType.DMA((COPIES,)),
            pltpu.SemaphoreType.DMA((COPIES,)),
            pltpu.SemaphoreType.DMA((2,)),
        ],
        compiler_params=pltpu.CompilerParams(
            collective_id=0, has_side_effects=True, vmem_limit_bytes=56 * 1024 * 1024
        ),
        name="sweep",
    )(theta, env_left, env_right, sector_dims, right_dims, mpo_on, mpo_coef, mix_index, weight_table)
    return (matvec[None], env_next)


def solution(mesh):
    split = Mesh(mesh.devices.reshape(4, 4, 4, 2), AXES)
    in_specs = (
        P(SECTOR, None, None),
        P(SECTOR),
        P(SECTOR),
        P(BOND, SECTOR, None, None),
        P(BOND, SECTOR, None, None),
        P(BOND),
        P(BOND),
        P(BOND, None),
        P(),
    )
    out_specs = (P(SECTOR, BOND, None), P(BOND, SECTOR, None, None))
    return jax.shard_map(on_device, mesh=split, in_specs=in_specs, out_specs=out_specs, check_vma=False)
```

```python
import math

import jax
import jax.numpy as jnp
from jax import lax
from jax.experimental import pallas as pl
from jax.experimental.pallas import tpu as pltpu
from jax.sharding import Mesh
from jax.sharding import PartitionSpec as P

AXES = ("bond_0", "bond_1", "sector_0", "sector_1")
BOND = ("bond_0", "bond_1")
SECTOR = ("sector_0", "sector_1")
MESH = pl.DeviceIdType.MESH
F32 = jnp.float32
BF16 = jnp.bfloat16

N = 768
BLK = 48
PIECES = 6
EARLY = 4
HOPS = 3
ORDER = (3, 0, 1, 4, 5, 2)
PIECE = N // PIECES
TILE = 256

RELAY_UP, RELAY_DOWN, UP_B, DOWN_A, UP_A, DOWN_B = range(6)
RS_Z = 6
AG_Z = 9
AG_UP = 12
AG_DOWN = 16
FWD = 20
SUM_CORE = 24
SUM_Y = 25
SUM_X = 28
SUM_Z = 31
HALO_UP = 34
HALO_DOWN = HALO_UP + PIECES
HOP_UP = HALO_DOWN + PIECES
HOP_DOWN = HOP_UP + HOPS
COPIES = HOP_DOWN + HOPS


def body(
    theta_h, left_h, right_h, rows_h, cols_h, on_h, coef_h, index_h, table_h,
    matvec_o, half_o, unit_o, square_o,
    rows_s, cols_s, on_s, coef_s, index_s, table_s,
    live, left, right, low, high, via_up, via_down, acc, relay_out, relay_in, side_out, from_left, from_right,
    z_out, z_in, unit, part, part_in, mixed, half,
    small_sem, load_sem, send_sem, recv_sem, store_sem,
):
    x = lax.axis_index("bond_0")
    z = lax.axis_index("bond_1")
    y = lax.axis_index("sector_0")
    c = lax.axis_index("sector_1")

    def at_x(d):
        return {"bond_0": lax.rem(x + d, 4)}

    def at_z(d):
        return {"bond_1": lax.rem(z + d, 4)}

    def at_y(d):
        return {"sector_0": lax.rem(y + d, 4)}

    other = {"sector_1": 1 - c}
    bond = x * 4 + z
    above = lax.rem(bond + 1, 16)
    below = lax.rem(bond + 15, 16)
    up = {"bond_0": above // 4, "bond_1": lax.rem(above, 4)}
    down = {"bond_0": below // 4, "bond_1": lax.rem(below, 4)}
    peers = [at_x(1), at_x(2), at_x(3), at_z(1), at_z(2), at_z(3), at_y(1), at_y(2), at_y(3), other, up, down]

    def remote(i, src, dst, device):
        return pltpu.make_async_remote_copy(
            src_ref=src, dst_ref=dst, send_sem=send_sem.at[i], recv_sem=recv_sem.at[i],
            device_id=device, device_id_type=MESH,
        )

    loads = [
        pltpu.make_async_copy(theta_h.at[0], live, load_sem.at[0]),
        pltpu.make_async_copy(left_h.at[0, 0], left.at[0], load_sem.at[1]),
        pltpu.make_async_copy(left_h.at[1, 0], left.at[1], load_sem.at[2]),
        pltpu.make_async_copy(right_h.at[0, 0], right.at[0], load_sem.at[3]),
        pltpu.make_async_copy(right_h.at[1, 0], right.at[1], load_sem.at[4]),
    ]
    smalls = [
        pltpu.make_async_copy(source, target, small_sem.at[n])
        for n, (source, target) in enumerate(
            [(rows_h, rows_s), (cols_h, cols_s), (on_h, on_s), (coef_h, coef_s), (index_h, index_s), (table_h, table_s)]
        )
    ]
    barrier = pltpu.get_barrier_semaphore()
    for peer in peers:
        pl.semaphore_signal(barrier, inc=1, device_id=peer, device_id_type=MESH)
    for load in smalls + loads:
        load.start()
    pl.semaphore_wait(barrier, len(peers))

    def rows_of(p):
        return pl.ds(p * PIECE, PIECE)

    def up_first(p, via):
        target = via_up.at[p] if via else low.at[rows_of(p)]
        return remote(HALO_UP + p, left_h.at[1, 0, rows_of(p)], target, at_z(1) if p < HOPS else up)

    def down_first(p, via):
        target = via_down.at[p] if via else high.at[rows_of(p)]
        return remote(HALO_DOWN + p, left_h.at[0, 0, rows_of(p)], target, at_z(3) if p < HOPS else down)

    def up_hop(p):
        return remote(HOP_UP + p, via_up.at[p], low.at[rows_of(p)], at_x(1))

    def down_hop(p):
        return remote(HOP_DOWN + p, via_down.at[p], high.at[rows_of(p)], at_x(3))

    def start_up(p):
        if p < HOPS:
            pl.when(z == 3)(lambda: up_first(p, True).start())
            pl.when(z != 3)(lambda: up_first(p, False).start())
        else:
            up_first(p, False).start()

    def start_down(p):
        if p < HOPS:
            pl.when(z == 0)(lambda: down_first(p, True).start())
            pl.when(z != 0)(lambda: down_first(p, False).start())
        else:
            down_first(p, False).start()

    def forward(p):
        @pl.when(z == 0)
        def _():
            up_first(p, True).wait_recv()
            up_hop(p).start()

        @pl.when(z == 3)
        def _():
            down_first(p, True).wait_recv()
            down_hop(p).start()

    def halo_arrive(p):
        if p < HOPS:
            pl.when(z == 0)(lambda: up_hop(p).wait_recv())
            pl.when(z != 0)(lambda: up_first(p, False).wait_recv())
            pl.when(z == 3)(lambda: down_hop(p).wait_recv())
            pl.when(z != 3)(lambda: down_first(p, False).wait_recv())
        else:
            up_first(p, False).wait_recv()
            down_first(p, False).wait_recv()

    for p in range(EARLY):
        start_up(p)
        start_down(p)

    for load in smalls:
        load.wait()
    row_dim = rows_s[0]
    col_dim = cols_s[0]
    loads[0].wait()

    @pl.loop(0, N // 128)
    def _(i):
        rows = pl.ds(pl.multiple_of(i * 128, 128), 128)
        row_id = lax.broadcasted_iota(jnp.int32, (128, N), 0) + i * 128
        col_id = lax.broadcasted_iota(jnp.int32, (128, N), 1)
        keep = (row_id < row_dim) & (col_id < col_dim)
        live[rows] = jnp.where(keep, live[rows].astype(F32), 0.0).astype(BF16)

    for load in loads[1:]:
        load.wait()

    gains = [coef_s[w] * on_s[w].astype(F32) for w in range(2)]

    relay_up = remote(RELAY_UP, relay_out.at[0], relay_in.at[0], at_x(1))
    relay_down = remote(RELAY_DOWN, relay_out.at[1], relay_in.at[1], at_x(3))
    up_b = remote(UP_B, side_out.at[0, pl.ds(2, 2)], from_left.at[pl.ds(2, 2)], at_x(1))
    up_a = remote(UP_A, side_out.at[0, pl.ds(0, 2)], from_left.at[pl.ds(0, 2)], at_x(1))
    down_a = remote(DOWN_A, side_out.at[1, pl.ds(0, 2)], from_right.at[pl.ds(0, 2)], at_x(3))
    down_b = remote(DOWN_B, side_out.at[1, pl.ds(2, 2)], from_right.at[pl.ds(2, 2)], at_x(3))

    @pl.loop(0, 4)
    def _(i):
        owner = lax.rem(x + 2 + i, 4)
        rows = pl.ds(pl.multiple_of(owner * 192, 64), 192)
        total = None
        for w in range(2):
            applied = jnp.dot(left[w, rows, :], live[...], preferred_element_type=F32).astype(BF16)
            term = gains[w] * lax.dot_general(
                applied, right[w], (((1,), (1,)), ((), ())), preferred_element_type=F32
            )
            total = term if total is None else total + term
        acc[i] = total.reshape(4, BLK, N)

        @pl.when(i == 0)
        def _():
            relay_out[0] = acc[0, 0:2].astype(BF16)
            relay_up.start()
            relay_out[1] = acc[0, 2:4].astype(BF16)
            relay_down.start()

        @pl.when(i == 1)
        def _():
            side_out[1, 0:2] = acc[1, 0:2].astype(BF16)
            down_a.start()

        @pl.when(i == 3)
        def _():
            side_out[0, 2:4] = acc[3, 2:4].astype(BF16)
            up_b.start()

    relay_up.wait_recv()
    side_out[0, 0:2] = (acc[3, 0:2] + relay_in[0].astype(F32)).astype(BF16)
    up_a.start()
    relay_down.wait_recv()
    side_out[1, 2:4] = (acc[1, 2:4] + relay_in[1].astype(F32)).astype(BF16)
    down_b.start()

    up_b.wait_recv()
    down_a.wait_recv()
    up_a.wait_recv()
    down_b.wait_recv()

    @pl.when(z == 3)
    def _():
        for p in range(EARLY, PIECES):
            start_up(p)

    @pl.when(z == 0)
    def _():
        for p in range(EARLY, PIECES):
            start_down(p)

    forward(0)
    forward(1)

    def row_sum(j):
        return acc[2, j] + from_left[j].astype(F32) + from_right[j].astype(F32)

    rs_z = {d: remote(RS_Z + d - 1, z_out.at[d - 1], z_in.at[d - 1], at_z(d)) for d in (1, 2, 3)}
    for d in (2, 1, 3):
        z_out[d - 1] = row_sum(lax.rem(z + d, 4)).astype(BF16)
        rs_z[d].start()
    mine = row_sum(z)
    for d in (1, 3, 2):
        rs_z[d].wait_recv()
        mine = mine + z_in[d - 1].astype(F32)
    row_id = lax.broadcasted_iota(jnp.int32, (BLK, N), 0) + bond * BLK
    col_id = lax.broadcasted_iota(jnp.int32, (BLK, N), 1)
    mine = jnp.where((row_id < row_dim) & (col_id < col_dim), mine, 0.0)
    rounded = mine.astype(BF16)
    unit[bond] = rounded

    def block(cx, r):
        return unit.at[lax.rem(x + cx, 4) * 4 + lax.rem(z + 4 - r, 4)]

    ag_z = {d: remote(AG_Z + d - 1, unit.at[bond], unit.at[bond], at_z(d)) for d in (1, 2, 3)}
    for d in (2, 1, 3):
        ag_z[d].start()
    ag_up = [remote(AG_UP + r, block(0, r), block(0, r), at_x(1)) for r in range(4)]
    ag_down = [remote(AG_DOWN + r, block(0, r), block(0, r), at_x(3)) for r in range(4)]
    ag_up[0].start()
    ag_down[0].start()

    matvec_o[...] = rounded
    square = mine * mine
    tile = jnp.zeros((8, 128), F32)
    for a in range(BLK // 8):
        for b in range(N // 128):
            tile = tile + square[a * 8 : a * 8 + 8, b * 128 : b * 128 + 128]
    part[0] = tile

    def spread(i, slot, devices):
        return [
            remote(i + n, part.at[slot], part_in.at[i - SUM_CORE + n], device) for n, device in enumerate(devices)
        ]

    sums = [
        spread(SUM_CORE, 0, [other]),
        spread(SUM_Y, 1, [at_y(1), at_y(2), at_y(3)]),
        spread(SUM_X, 2, [at_x(1), at_x(2), at_x(3)]),
        spread(SUM_Z, 3, [at_z(1), at_z(2), at_z(3)]),
    ]
    firsts = [0, 1, 4, 7]

    def sum_start(stage):
        for copy in sums[stage]:
            copy.start()

    def sum_finish(stage):
        total = part[stage]
        for n, copy in enumerate(sums[stage]):
            copy.wait_recv()
            total = total + part_in[firsts[stage] + n]
        part[stage + 1] = total

    sum_start(0)
    for d in (1, 3, 2):
        remote(AG_Z + d - 1, block(0, d), block(0, d), at_z(d)).wait_recv()
        ag_up[d].start()
        ag_down[d].start()

    @pl.when(z != 3)
    def _():
        for p in range(EARLY, PIECES):
            start_up(p)

    @pl.when(z != 0)
    def _():
        for p in range(EARLY, PIECES):
            start_down(p)

    sum_finish(0)
    sum_start(1)

    w_gain = [[table_s[index_s[w, k]] for k in range(3)] for w in range(2)]
    low_gain = jnp.where(bond > 0, w_gain[0][0], 0.0)
    high_gain = jnp.where(bond < 15, w_gain[1][2], 0.0)

    def mix(p):
        rows = rows_of(p)
        halo_arrive(p)
        here = left[0, rows].astype(F32)
        there = left[1, rows].astype(F32)
        mixed[0, rows] = (low_gain * low[rows].astype(F32) + w_gain[0][1] * here + w_gain[0][2] * there).astype(BF16)
        mixed[1, rows] = (w_gain[1][0] * here + w_gain[1][1] * there + high_gain * high[rows].astype(F32)).astype(BF16)

    def arrive(i, cx, r):
        remote(i + r, block(cx, r), block(cx, r), at_x(1)).wait_recv()

    fwd = {
        0: remote(FWD, block(3, 0), block(3, 0), at_x(1)),
        3: remote(FWD + 3, block(3, 3), block(3, 3), at_x(1)),
        1: remote(FWD + 1, block(1, 1), block(1, 1), at_x(3)),
        2: remote(FWD + 2, block(1, 2), block(1, 2), at_x(3)),
    }
    arrive(AG_UP, 3, 0)
    fwd[0].start()
    arrive(AG_DOWN, 1, 0)
    arrive(AG_DOWN, 1, 1)
    fwd[1].start()
    arrive(AG_UP, 3, 1)
    sum_finish(1)
    sum_start(2)
    arrive(AG_UP, 3, 3)
    fwd[3].start()
    arrive(AG_DOWN, 1, 3)
    arrive(AG_DOWN, 1, 2)
    fwd[2].start()
    arrive(AG_UP, 3, 2)
    sum_finish(2)
    sum_start(3)
    forward(2)
    for p in ORDER[:4]:
        mix(p)
    sum_finish(3)
    square_o[...] = part[4]
    square_total = jnp.sum(part[4])
    scale = lax.rsqrt(jnp.full((1, N), square_total * (1.0 / (8 * N * N)) + 1e-06, F32))
    mix(ORDER[4])
    for r in range(4):
        remote(FWD + r, block(2, r), block(2, r), at_x(1)).wait_recv()
    unit_store = pltpu.make_async_copy(unit, unit_o, store_sem.at[2 * PIECES])
    unit_store.start()

    stores = []
    for p in ORDER:
        rows = rows_of(p)
        if p == ORDER[5]:
            mix(p)
        product = jnp.dot(mixed[:, rows, :].reshape(2 * PIECE, N), unit[...].reshape(N, N), preferred_element_type=F32)
        half[:, rows] = (product * scale).astype(BF16).reshape(2, PIECE, N)
        for w in range(2):
            stores.append(pltpu.make_async_copy(half.at[w, rows], half_o.at[w, rows], store_sem.at[2 * p + w]))
            stores[-1].start()

    for copy in (relay_up, relay_down, up_a, up_b, down_a, down_b):
        copy.wait_send()
    for d in (1, 2, 3):
        rs_z[d].wait_send()
        ag_z[d].wait_send()
    for r in range(4):
        ag_up[r].wait_send()
        ag_down[r].wait_send()
        fwd[r].wait_send()
    for stage in sums:
        for copy in stage:
            copy.wait_send()
    for p in range(PIECES):
        up_first(p, False).wait_send()
        down_first(p, False).wait_send()
    for p in range(HOPS):
        pl.when(z == 0)(lambda: up_hop(p).wait_send())
        pl.when(z == 3)(lambda: down_hop(p).wait_send())
    for store in stores:
        store.wait()
    unit_store.wait()


def last_product(matvec_h, half_h, unit_h, square_h, matvec_o, env_o, matvec, half, unit, square, grown, sem):
    loads = [
        pltpu.make_async_copy(unit_h, unit, sem.at[0]),
        pltpu.make_async_copy(half_h.at[0], half.at[0], sem.at[1]),
        pltpu.make_async_copy(half_h.at[1], half.at[1], sem.at[2]),
        pltpu.make_async_copy(square_h, square, sem.at[3]),
        pltpu.make_async_copy(matvec_h, matvec, sem.at[4]),
    ]
    for load in loads:
        load.start()
    loads[3].wait()
    factor = lax.rsqrt(jnp.full((1, N), jnp.sum(square[...]) * (1.0 / (8 * N * N)) + 1e-06, F32)) * (1.0 / math.sqrt(N))
    loads[4].wait()
    stores = [pltpu.make_async_copy(matvec, matvec_o, sem.at[5])]
    stores[0].start()
    loads[0].wait()
    for w in range(2):
        loads[1 + w].wait()
        for k in range(N // TILE):
            rows = pl.ds(k * TILE, TILE)
            side = unit[:, :, k * TILE : (k + 1) * TILE].reshape(N, TILE)
            product = lax.dot_general(side, half[w], (((0,), (0,)), ((), ())), preferred_element_type=F32)
            grown[w, rows] = (product * factor).astype(BF16)
            stores.append(pltpu.make_async_copy(grown.at[w, rows], env_o.at[w, 0, rows], sem.at[6 + 3 * w + k]))
            stores[-1].start()
    for store in stores:
        store.wait()


def on_device(
    theta, sector_dims, right_dims, env_left, env_right, mpo_on, mpo_coef, mix_index, weight_table
):
    hbm = pl.BlockSpec(memory_space=pl.ANY)
    vmem = pl.BlockSpec(memory_space=pltpu.VMEM)
    matvec, half, unit, square = pl.pallas_call(
        body,
        out_shape=(
            jax.ShapeDtypeStruct((BLK, N), BF16),
            jax.ShapeDtypeStruct((2, N, N), BF16),
            jax.ShapeDtypeStruct((16, BLK, N), BF16),
            jax.ShapeDtypeStruct((8, 128), F32),
        ),
        in_specs=[hbm] * 9,
        out_specs=(vmem, hbm, hbm, vmem),
        scratch_shapes=[
            pltpu.SMEM((1,), jnp.int32),
            pltpu.SMEM((1,), jnp.int32),
            pltpu.SMEM((2,), jnp.int32),
            pltpu.SMEM((2,), F32),
            pltpu.SMEM((2, 3), jnp.int32),
            pltpu.SMEM((8,), F32),
            pltpu.VMEM((N, N), BF16),
            pltpu.VMEM((2, N, N), BF16),
            pltpu.VMEM((2, N, N), BF16),
            pltpu.VMEM((N, N), BF16),
            pltpu.VMEM((N, N), BF16),
            pltpu.VMEM((HOPS, PIECE, N), BF16),
            pltpu.VMEM((HOPS, PIECE, N), BF16),
            pltpu.VMEM((4, 4, BLK, N), F32),
            pltpu.VMEM((2, 2, BLK, N), BF16),
            pltpu.VMEM((2, 2, BLK, N), BF16),
            pltpu.VMEM((2, 4, BLK, N), BF16),
            pltpu.VMEM((4, BLK, N), BF16),
            pltpu.VMEM((4, BLK, N), BF16),
            pltpu.VMEM((3, BLK, N), BF16),
            pltpu.VMEM((3, BLK, N), BF16),
            pltpu.VMEM((16, BLK, N), BF16),
            pltpu.VMEM((5, 8, 128), F32),
            pltpu.VMEM((10, 8, 128), F32),
            pltpu.VMEM((2, N, N), BF16),
            pltpu.VMEM((2, N, N), BF16),
            pltpu.SemaphoreType.DMA((6,)),
            pltpu.SemaphoreType.DMA((5,)),
            pltpu.SemaphoreType.DMA((COPIES,)),
            pltpu.SemaphoreType.DMA((COPIES,)),
            pltpu.SemaphoreType.DMA((2 * PIECES + 1,)),
        ],
        compiler_params=pltpu.CompilerParams(
            collective_id=0, has_side_effects=True, vmem_limit_bytes=56 * 1024 * 1024
        ),
        name="sweep",
    )(theta, env_left, env_right, sector_dims, right_dims, mpo_on, mpo_coef, mix_index, weight_table)
    matvec, env_next = pl.pallas_call(
        last_product,
        out_shape=(jax.ShapeDtypeStruct((BLK, N), BF16), jax.ShapeDtypeStruct(env_left.shape, BF16)),
        in_specs=[hbm] * 4,
        out_specs=(hbm, hbm),
        scratch_shapes=[
            pltpu.VMEM((BLK, N), BF16),
            pltpu.VMEM((2, N, N), BF16),
            pltpu.VMEM((16, BLK, N), BF16),
            pltpu.VMEM((8, 128), F32),
            pltpu.VMEM((2, N, N), BF16),
            pltpu.SemaphoreType.DMA((12,)),
        ],
        compiler_params=pltpu.CompilerParams(vmem_limit_bytes=56 * 1024 * 1024),
        name="last_product",
    )(matvec, half, unit, square)
    return (matvec[None], env_next)


def solution(mesh):
    split = Mesh(mesh.devices.reshape(4, 4, 4, 2), AXES)
    in_specs = (
        P(SECTOR, None, None),
        P(SECTOR),
        P(SECTOR),
        P(BOND, SECTOR, None, None),
        P(BOND, SECTOR, None, None),
        P(BOND),
        P(BOND),
        P(BOND, None),
        P(),
    )
    out_specs = (P(SECTOR, BOND, None), P(BOND, SECTOR, None, None))
    return jax.shard_map(on_device, mesh=split, in_specs=in_specs, out_specs=out_specs, check_vma=False)
```

```python
import math

import jax
import jax.numpy as jnp
from jax import lax
from jax.experimental import pallas as pl
from jax.experimental.pallas import tpu as pltpu
from jax.sharding import Mesh
from jax.sharding import PartitionSpec as P

AXES = ("bond_0", "bond_1", "sector_0", "sector_1")
BOND = ("bond_0", "bond_1")
SECTOR = ("sector_0", "sector_1")
MESH = pl.DeviceIdType.MESH
F32 = jnp.float32
BF16 = jnp.bfloat16

N = 768
BLK = 48
PIECES = 6
EARLY = 4
HOPS = 3
ORDER = (3, 0, 1, 4, 5, 2)
LIFT = 1024.0
PIECE = N // PIECES
TILE = 256

RELAY_UP, RELAY_DOWN, UP_B, DOWN_A, UP_A, DOWN_B = range(6)
RS_Z = 6
AG_Z = 9
AG_UP = 12
AG_DOWN = 16
FWD = 20
SUM_CORE = 24
SUM_Y = 25
HALO_UP = 28
HALO_DOWN = HALO_UP + PIECES
HOP_UP = HALO_DOWN + PIECES
HOP_DOWN = HOP_UP + PIECES
COPIES = HOP_DOWN + PIECES


def body(
    theta_h, left_h, right_h, rows_h, cols_h, on_h, coef_h, index_h, table_h,
    matvec_o, half_o, turned_o, square_o,
    rows_s, cols_s, on_s, coef_s, index_s, table_s,
    live, left, right, low, high, via_up, via_down, acc, relay_out, relay_in, side_out, from_left, from_right,
    z_out, z_in, unit, turned, part, part_in, mixed, half,
    small_sem, load_sem, send_sem, recv_sem, store_sem,
):
    x = lax.axis_index("bond_0")
    z = lax.axis_index("bond_1")
    y = lax.axis_index("sector_0")
    c = lax.axis_index("sector_1")

    def at_x(d):
        return {"bond_0": lax.rem(x + d, 4)}

    def at_z(d):
        return {"bond_1": lax.rem(z + d, 4)}

    def at_y(d):
        return {"sector_0": lax.rem(y + d, 4)}

    other = {"sector_1": 1 - c}
    bond = x * 4 + z
    peers = [at_x(1), at_x(3), at_z(1), at_z(2), at_z(3), at_y(1), at_y(2), at_y(3), other]

    def remote(i, src, dst, device):
        return pltpu.make_async_remote_copy(
            src_ref=src, dst_ref=dst, send_sem=send_sem.at[i], recv_sem=recv_sem.at[i],
            device_id=device, device_id_type=MESH,
        )

    loads = [
        pltpu.make_async_copy(theta_h.at[0], live, load_sem.at[0]),
        pltpu.make_async_copy(left_h.at[0, 0], left.at[0], load_sem.at[1]),
        pltpu.make_async_copy(left_h.at[1, 0], left.at[1], load_sem.at[2]),
        pltpu.make_async_copy(right_h.at[0, 0], right.at[0], load_sem.at[3]),
        pltpu.make_async_copy(right_h.at[1, 0], right.at[1], load_sem.at[4]),
    ]
    smalls = [
        pltpu.make_async_copy(source, target, small_sem.at[n])
        for n, (source, target) in enumerate(
            [(rows_h, rows_s), (cols_h, cols_s), (on_h, on_s), (coef_h, coef_s), (index_h, index_s), (table_h, table_s)]
        )
    ]
    barrier = pltpu.get_barrier_semaphore()
    for peer in peers:
        pl.semaphore_signal(barrier, inc=1, device_id=peer, device_id_type=MESH)
    for load in smalls + loads:
        load.start()
    pl.semaphore_wait(barrier, len(peers))

    def rows_of(p):
        return pl.ds(p * PIECE, PIECE)

    class Side:
        def __init__(self, channel, last, step, target, via, first, hop):
            self.channel, self.last, self.step, self.target, self.via = channel, last, step, target, via
            self.first_sem, self.hop_sem, self.receiver = first, hop, 3 - last

        def source(self, p):
            return left_h.at[self.channel, 0, rows_of(p)]

        def along_z(self, p, source, target):
            return remote(self.first_sem + p, source, target, at_z(self.step))

        def along_x(self, p, source, target):
            return remote(self.hop_sem + p, source, target, at_x(self.step))

        def direct(self, p):
            return self.along_z(p, self.source(p), self.target.at[rows_of(p)])

        def leave(self, p):
            if p < HOPS:
                return self.along_z(p, self.source(p), self.via.at[p])
            return self.along_x(p, self.source(p), self.via.at[p])

        def onward(self, p):
            if p < HOPS:
                return self.along_x(p, self.via.at[p], self.target.at[rows_of(p)])
            return self.along_z(p, self.via.at[p], self.target.at[rows_of(p)])

        def start(self, p):
            pl.when(z == self.last)(lambda: self.leave(p).start())
            pl.when(z != self.last)(lambda: self.direct(p).start())

        def relay(self, p):
            @pl.when(z == (self.receiver if p < HOPS else self.last))
            def _():
                self.leave(p).wait_recv()
                self.onward(p).start()

        def arrive(self, p):
            if p < HOPS:
                pl.when(z == self.receiver)(lambda: self.onward(p).wait_recv())
                pl.when(z != self.receiver)(lambda: self.direct(p).wait_recv())
            else:
                self.direct(p).wait_recv()

        def sent(self, p):
            self.direct(p).wait_send()
            if p < HOPS:
                pl.when(z == self.receiver)(lambda: self.onward(p).wait_send())
            else:
                pl.when(z == self.last)(lambda: self.leave(p).wait_send())

    rising = Side(1, 3, 1, low, via_up, HALO_UP, HOP_UP)
    falling = Side(0, 0, 3, high, via_down, HALO_DOWN, HOP_DOWN)

    def forward(p):
        rising.relay(p)
        falling.relay(p)

    for p in range(EARLY):
        rising.start(p)
        falling.start(p)

    for load in smalls:
        load.wait()
    row_dim = rows_s[0]
    col_dim = cols_s[0]
    loads[0].wait()

    @pl.loop(0, N // 128)
    def _(i):
        rows = pl.ds(pl.multiple_of(i * 128, 128), 128)
        row_id = lax.broadcasted_iota(jnp.int32, (128, N), 0) + i * 128
        col_id = lax.broadcasted_iota(jnp.int32, (128, N), 1)
        keep = (row_id < row_dim) & (col_id < col_dim)
        live[rows] = jnp.where(keep, live[rows].astype(F32), 0.0).astype(BF16)

    for load in loads[1:]:
        load.wait()

    gains = [coef_s[w] * on_s[w].astype(F32) for w in range(2)]

    relay_up = remote(RELAY_UP, relay_out.at[0], relay_in.at[0], at_x(1))
    relay_down = remote(RELAY_DOWN, relay_out.at[1], relay_in.at[1], at_x(3))
    up_b = remote(UP_B, side_out.at[0, pl.ds(2, 2)], from_left.at[pl.ds(2, 2)], at_x(1))
    up_a = remote(UP_A, side_out.at[0, pl.ds(0, 2)], from_left.at[pl.ds(0, 2)], at_x(1))
    down_a = remote(DOWN_A, side_out.at[1, pl.ds(0, 2)], from_right.at[pl.ds(0, 2)], at_x(3))
    down_b = remote(DOWN_B, side_out.at[1, pl.ds(2, 2)], from_right.at[pl.ds(2, 2)], at_x(3))

    @pl.loop(0, 4)
    def _(i):
        owner = lax.rem(x + 2 + i, 4)
        rows = pl.ds(pl.multiple_of(owner * 192, 64), 192)
        total = None
        for w in range(2):
            applied = jnp.dot(left[w, rows, :], live[...], preferred_element_type=F32).astype(BF16)
            term = gains[w] * lax.dot_general(
                applied, right[w], (((1,), (1,)), ((), ())), preferred_element_type=F32
            )
            total = term if total is None else total + term
        acc[i] = total.reshape(4, BLK, N)

        @pl.when(i == 0)
        def _():
            relay_out[0] = acc[0, 0:2].astype(BF16)
            relay_up.start()
            relay_out[1] = acc[0, 2:4].astype(BF16)
            relay_down.start()

        @pl.when(i == 1)
        def _():
            side_out[1, 0:2] = acc[1, 0:2].astype(BF16)
            down_a.start()

        @pl.when(i == 3)
        def _():
            side_out[0, 2:4] = acc[3, 2:4].astype(BF16)
            up_b.start()

    relay_up.wait_recv()
    side_out[0, 0:2] = (acc[3, 0:2] + relay_in[0].astype(F32)).astype(BF16)
    up_a.start()
    relay_down.wait_recv()
    side_out[1, 2:4] = (acc[1, 2:4] + relay_in[1].astype(F32)).astype(BF16)
    down_b.start()

    up_b.wait_recv()
    down_a.wait_recv()
    up_a.wait_recv()
    down_b.wait_recv()

    for p in range(EARLY, PIECES):
        pl.when(z == 3)(lambda: rising.leave(p).start())
        pl.when(z == 0)(lambda: falling.leave(p).start())
    for p in (0, 1, 3):
        forward(p)

    def row_sum(j):
        return acc[2, j] + from_left[j].astype(F32) + from_right[j].astype(F32)

    rs_z = {d: remote(RS_Z + d - 1, z_out.at[d - 1], z_in.at[d - 1], at_z(d)) for d in (1, 2, 3)}
    for d in (2, 1, 3):
        z_out[d - 1] = row_sum(lax.rem(z + d, 4)).astype(BF16)
        rs_z[d].start()
    mine = row_sum(z)
    for d in (1, 3, 2):
        rs_z[d].wait_recv()
        mine = mine + z_in[d - 1].astype(F32)
    row_id = lax.broadcasted_iota(jnp.int32, (BLK, N), 0) + bond * BLK
    col_id = lax.broadcasted_iota(jnp.int32, (BLK, N), 1)
    mine = jnp.where((row_id < row_dim) & (col_id < col_dim), mine, 0.0)
    rounded = mine.astype(BF16)
    unit[bond] = rounded

    def block(cx, r):
        return unit.at[lax.rem(x + cx, 4) * 4 + lax.rem(z + 4 - r, 4)]

    ag_z = {d: remote(AG_Z + d - 1, unit.at[bond], unit.at[bond], at_z(d)) for d in (1, 2, 3)}
    for d in (2, 1, 3):
        ag_z[d].start()
    ag_up = [remote(AG_UP + r, block(0, r), block(0, r), at_x(1)) for r in range(4)]
    ag_down = [remote(AG_DOWN + r, block(0, r), block(0, r), at_x(3)) for r in range(4)]
    ag_up[0].start()
    ag_down[0].start()

    matvec_o[...] = rounded
    for d in (1, 3, 2):
        remote(AG_Z + d - 1, block(0, d), block(0, d), at_z(d)).wait_recv()
        ag_up[d].start()
        ag_down[d].start()

    for p in range(EARLY, PIECES):
        pl.when(z != 3)(lambda: rising.direct(p).start())
        pl.when(z != 0)(lambda: falling.direct(p).start())

    w_gain = [[table_s[index_s[w, k]] for k in range(3)] for w in range(2)]
    low_gain = jnp.where(bond > 0, w_gain[0][0], 0.0)
    high_gain = jnp.where(bond < 15, w_gain[1][2], 0.0)

    def mix(p):
        rows = rows_of(p)
        rising.arrive(p)
        falling.arrive(p)
        here = left[0, rows].astype(F32)
        there = left[1, rows].astype(F32)
        mixed[0, rows] = (low_gain * low[rows].astype(F32) + w_gain[0][1] * here + w_gain[0][2] * there).astype(BF16)
        mixed[1, rows] = (w_gain[1][0] * here + w_gain[1][1] * there + high_gain * high[rows].astype(F32)).astype(BF16)

    def arrive(i, cx, r):
        remote(i + r, block(cx, r), block(cx, r), at_x(1)).wait_recv()

    fwd = {
        0: remote(FWD, block(3, 0), block(3, 0), at_x(1)),
        3: remote(FWD + 3, block(3, 3), block(3, 3), at_x(1)),
        1: remote(FWD + 1, block(1, 1), block(1, 1), at_x(3)),
        2: remote(FWD + 2, block(1, 2), block(1, 2), at_x(3)),
    }
    def squares(cx):
        total = jnp.zeros((16, 128), F32)
        for r in range(4):
            value = block(cx, r)[...].astype(F32)
            value = value * value
            for a in range(BLK // 16):
                for b in range(N // 128):
                    total = total + value[a * 16 : a * 16 + 16, b * 128 : b * 128 + 128]
        return total[:8] + total[8:]

    arrive(AG_UP, 3, 0)
    fwd[0].start()
    arrive(AG_DOWN, 1, 0)
    arrive(AG_DOWN, 1, 1)
    fwd[1].start()
    forward(4)
    arrive(AG_UP, 3, 1)
    arrive(AG_UP, 3, 3)
    fwd[3].start()
    arrive(AG_DOWN, 1, 3)
    arrive(AG_DOWN, 1, 2)
    fwd[2].start()
    forward(5)
    forward(2)
    arrive(AG_UP, 3, 2)
    part[0] = squares(0) + squares(1) + squares(3)
    for p in ORDER[:5]:
        mix(p)
    for r in range(4):
        remote(FWD + r, block(2, r), block(2, r), at_x(1)).wait_recv()

    part[0] = part[0] + squares(2)
    sum_core = remote(SUM_CORE, part.at[0], part_in.at[0], other)
    sum_y = [remote(SUM_Y + n, part.at[1], part_in.at[1 + n], at_y(1 + n)) for n in range(3)]
    sum_core.start()

    stores = []

    def product(p):
        rows = rows_of(p)
        result = jnp.dot(mixed[:, rows, :].reshape(2 * PIECE, N), unit[...].reshape(N, N), preferred_element_type=F32)
        half[:, rows] = (result * LIFT).astype(BF16).reshape(2, PIECE, N)
        for w in range(2):
            stores.append(pltpu.make_async_copy(half.at[w, rows], half_o.at[w, rows], store_sem.at[2 * p + w]))
            stores[-1].start()

    for p in ORDER[:3]:
        product(p)
    sum_core.wait_recv()
    part[1] = part[0] + part_in[0]
    for copy in sum_y:
        copy.start()
    for p in ORDER[3:5]:
        product(p)
    for k in range(N // TILE):
        turned[k * TILE : (k + 1) * TILE] = unit[:, :, k * TILE : (k + 1) * TILE].reshape(N, TILE).T
    turned_store = pltpu.make_async_copy(turned, turned_o, store_sem.at[2 * PIECES])
    turned_store.start()
    for copy in sum_y:
        copy.wait_recv()
    square_o[...] = part[1] + part_in[1] + part_in[2] + part_in[3]
    mix(ORDER[5])
    product(ORDER[5])

    for copy in (relay_up, relay_down, up_a, up_b, down_a, down_b):
        copy.wait_send()
    for d in (1, 2, 3):
        rs_z[d].wait_send()
        ag_z[d].wait_send()
    for r in range(4):
        ag_up[r].wait_send()
        ag_down[r].wait_send()
        fwd[r].wait_send()
    for copy in [sum_core] + sum_y:
        copy.wait_send()
    for p in range(PIECES):
        rising.sent(p)
        falling.sent(p)
    for store in stores:
        store.wait()
    turned_store.wait()


def last_product(matvec_h, half_h, turned_h, square_h, matvec_o, env_o, matvec, half, turned, square, grown, sem):
    loads = [
        pltpu.make_async_copy(turned_h, turned, sem.at[0]),
        pltpu.make_async_copy(half_h.at[0], half.at[0], sem.at[1]),
        pltpu.make_async_copy(half_h.at[1], half.at[1], sem.at[2]),
        pltpu.make_async_copy(square_h, square, sem.at[3]),
        pltpu.make_async_copy(matvec_h, matvec, sem.at[4]),
    ]
    for load in loads:
        load.start()
    loads[3].wait()
    scale = lax.rsqrt(jnp.full((1, N), jnp.sum(square[...]) * (1.0 / (8 * N * N)) + 1e-06, F32))
    loads[4].wait()
    stores = [pltpu.make_async_copy(matvec, matvec_o, sem.at[5])]
    stores[0].start()
    loads[0].wait()
    for w in range(2):
        loads[1 + w].wait()
        for k in range(N // TILE):
            rows = pl.ds(k * TILE, TILE)
            product = jnp.dot(turned[rows], half[w], preferred_element_type=F32)
            grown[w, rows] = (product * scale * (scale * (1.0 / (LIFT * math.sqrt(N))))).astype(BF16)
            stores.append(pltpu.make_async_copy(grown.at[w, rows], env_o.at[w, 0, rows], sem.at[6 + 3 * w + k]))
            stores[-1].start()
    for store in stores:
        store.wait()


def on_device(
    theta, sector_dims, right_dims, env_left, env_right, mpo_on, mpo_coef, mix_index, weight_table
):
    hbm = pl.BlockSpec(memory_space=pl.ANY)
    vmem = pl.BlockSpec(memory_space=pltpu.VMEM)
    matvec, half, turned, square = pl.pallas_call(
        body,
        out_shape=(
            jax.ShapeDtypeStruct((BLK, N), BF16),
            jax.ShapeDtypeStruct((2, N, N), BF16),
            jax.ShapeDtypeStruct((N, N), BF16),
            jax.ShapeDtypeStruct((8, 128), F32),
        ),
        in_specs=[hbm] * 9,
        out_specs=(vmem, hbm, hbm, vmem),
        scratch_shapes=[
            pltpu.SMEM((1,), jnp.int32),
            pltpu.SMEM((1,), jnp.int32),
            pltpu.SMEM((2,), jnp.int32),
            pltpu.SMEM((2,), F32),
            pltpu.SMEM((2, 3), jnp.int32),
            pltpu.SMEM((8,), F32),
            pltpu.VMEM((N, N), BF16),
            pltpu.VMEM((2, N, N), BF16),
            pltpu.VMEM((2, N, N), BF16),
            pltpu.VMEM((N, N), BF16),
            pltpu.VMEM((N, N), BF16),
            pltpu.VMEM((PIECES, PIECE, N), BF16),
            pltpu.VMEM((PIECES, PIECE, N), BF16),
            pltpu.VMEM((4, 4, BLK, N), F32),
            pltpu.VMEM((2, 2, BLK, N), BF16),
            pltpu.VMEM((2, 2, BLK, N), BF16),
            pltpu.VMEM((2, 4, BLK, N), BF16),
            pltpu.VMEM((4, BLK, N), BF16),
            pltpu.VMEM((4, BLK, N), BF16),
            pltpu.VMEM((3, BLK, N), BF16),
            pltpu.VMEM((3, BLK, N), BF16),
            pltpu.VMEM((16, BLK, N), BF16),
            pltpu.VMEM((N, N), BF16),
            pltpu.VMEM((2, 8, 128), F32),
            pltpu.VMEM((4, 8, 128), F32),
            pltpu.VMEM((2, N, N), BF16),
            pltpu.VMEM((2, N, N), BF16),
            pltpu.SemaphoreType.DMA((6,)),
            pltpu.SemaphoreType.DMA((5,)),
            pltpu.SemaphoreType.DMA((COPIES,)),
            pltpu.SemaphoreType.DMA((COPIES,)),
            pltpu.SemaphoreType.DMA((2 * PIECES + 1,)),
        ],
        compiler_params=pltpu.CompilerParams(
            collective_id=0, has_side_effects=True, vmem_limit_bytes=56 * 1024 * 1024
        ),
        name="sweep",
    )(theta, env_left, env_right, sector_dims, right_dims, mpo_on, mpo_coef, mix_index, weight_table)
    matvec, env_next = pl.pallas_call(
        last_product,
        out_shape=(jax.ShapeDtypeStruct((BLK, N), BF16), jax.ShapeDtypeStruct(env_left.shape, BF16)),
        in_specs=[hbm] * 4,
        out_specs=(hbm, hbm),
        scratch_shapes=[
            pltpu.VMEM((BLK, N), BF16),
            pltpu.VMEM((2, N, N), BF16),
            pltpu.VMEM((N, N), BF16),
            pltpu.VMEM((8, 128), F32),
            pltpu.VMEM((2, N, N), BF16),
            pltpu.SemaphoreType.DMA((12,)),
        ],
        compiler_params=pltpu.CompilerParams(vmem_limit_bytes=56 * 1024 * 1024),
        name="last_product",
    )(matvec, half, turned, square)
    return (matvec[None], env_next)


def solution(mesh):
    split = Mesh(mesh.devices.reshape(4, 4, 4, 2), AXES)
    in_specs = (
        P(SECTOR, None, None),
        P(SECTOR),
        P(SECTOR),
        P(BOND, SECTOR, None, None),
        P(BOND, SECTOR, None, None),
        P(BOND),
        P(BOND),
        P(BOND, None),
        P(),
    )
    out_specs = (P(SECTOR, BOND, None), P(BOND, SECTOR, None, None))
    return jax.shard_map(on_device, mesh=split, in_specs=in_specs, out_specs=out_specs, check_vma=False)
```

```python
import math

import jax
import jax.numpy as jnp
from jax import lax
from jax.experimental import pallas as pl
from jax.experimental.pallas import tpu as pltpu
from jax.sharding import Mesh
from jax.sharding import PartitionSpec as P

AXES = ("bond_0", "bond_1", "sector_0", "sector_1")
BOND = ("bond_0", "bond_1")
SECTOR = ("sector_0", "sector_1")
MESH = pl.DeviceIdType.MESH
F32 = jnp.float32
BF16 = jnp.bfloat16

N = 768
BLK = 48
SIZES = (96, 128, 128, 128, 144, 144)
PIECES = len(SIZES)
LAST = SIZES[-1]
SPLIT = 3
FIRST = (3, 4, 5, 0)
SECOND = (1, 2)
LIFT = 1024.0
TILE = 256

CHUNKS = 3
WIDTH = N // CHUNKS

RELAY_UP, RELAY_DOWN, UP_B, DOWN_A, UP_A, DOWN_B = range(0, 6 * CHUNKS, CHUNKS)
RS_Z = 6 * CHUNKS
AG_Z = 9 * CHUNKS
AG_UP, AG_DOWN, FWD_UP, FWD_DOWN = range(12 * CHUNKS, 16 * CHUNKS, CHUNKS)
SUM_Z = 16 * CHUNKS
SUM_X = SUM_Z + 3
SUM_S = SUM_X + 3
HALO_UP = SUM_S + 7
HALO_DOWN = HALO_UP + PIECES
HOP_UP = HALO_DOWN + PIECES
HOP_DOWN = HOP_UP + PIECES
COPIES = HOP_DOWN + PIECES


def body(
    theta_h, left_h, right_h, rows_h, cols_h, on_h, coef_h, index_h, table_h,
    matvec_o, half_o, turned_o, square_o,
    rows_s, cols_s, on_s, coef_s, index_s, table_s,
    live, left, right, low, high, via_up, via_down, acc, relay_out, relay_in, side_out, from_left, from_right,
    z_out, z_in, unit, turned, part, part_in, mixed, half,
    small_sem, load_sem, send_sem, recv_sem, store_sem,
):
    x = lax.axis_index("bond_0")
    z = lax.axis_index("bond_1")
    y = lax.axis_index("sector_0")
    c = lax.axis_index("sector_1")

    def at_x(d):
        return {"bond_0": lax.rem(x + d, 4)}

    def at_z(d):
        return {"bond_1": lax.rem(z + d, 4)}

    def at_y(d):
        return {"sector_0": lax.rem(y + d, 4)}

    other = {"sector_1": 1 - c}
    bond = x * 4 + z
    sectors = [other] + [at_y(d) for d in (1, 2, 3)] + [{**at_y(d), **other} for d in (1, 2, 3)]
    peers = [at_x(1), at_x(2), at_x(3), at_z(1), at_z(2), at_z(3)] + sectors

    def remote(i, src, dst, device):
        return pltpu.make_async_remote_copy(
            src_ref=src, dst_ref=dst, send_sem=send_sem.at[i], recv_sem=recv_sem.at[i],
            device_id=device, device_id_type=MESH,
        )

    loads = [
        pltpu.make_async_copy(theta_h.at[0], live, load_sem.at[0]),
        pltpu.make_async_copy(left_h.at[0, 0], left.at[0], load_sem.at[1]),
        pltpu.make_async_copy(left_h.at[1, 0], left.at[1], load_sem.at[2]),
        pltpu.make_async_copy(right_h.at[0, 0], right.at[0], load_sem.at[3]),
        pltpu.make_async_copy(right_h.at[1, 0], right.at[1], load_sem.at[4]),
    ]
    smalls = [
        pltpu.make_async_copy(source, target, small_sem.at[n])
        for n, (source, target) in enumerate(
            [(rows_h, rows_s), (cols_h, cols_s), (on_h, on_s), (coef_h, coef_s), (index_h, index_s), (table_h, table_s)]
        )
    ]
    barrier = pltpu.get_barrier_semaphore()
    for peer in peers:
        pl.semaphore_signal(barrier, inc=1, device_id=peer, device_id_type=MESH)
    for load in smalls + loads:
        load.start()
    pl.semaphore_wait(barrier, len(peers))

    def rows_of(p):
        return pl.ds(sum(SIZES[:p]), SIZES[p])

    class Side:
        def __init__(self, channel, last, step, target, via, first, hop):
            self.channel, self.last, self.step, self.target, self.via = channel, last, step, target, via
            self.first_sem, self.hop_sem, self.receiver = first, hop, 3 - last

        def stop(self, p):
            return self.via.at[p, pl.ds(0, SIZES[p])]

        def source(self, p):
            return left_h.at[self.channel, 0, rows_of(p)]

        def along_z(self, p, source, target):
            return remote(self.first_sem + p, source, target, at_z(self.step))

        def along_x(self, p, source, target):
            return remote(self.hop_sem + p, source, target, at_x(self.step))

        def direct(self, p):
            return self.along_z(p, self.source(p), self.target.at[rows_of(p)])

        def leave(self, p):
            if p >= SPLIT:
                return self.along_z(p, self.source(p), self.stop(p))
            return self.along_x(p, self.source(p), self.stop(p))

        def onward(self, p):
            if p >= SPLIT:
                return self.along_x(p, self.stop(p), self.target.at[rows_of(p)])
            return self.along_z(p, self.stop(p), self.target.at[rows_of(p)])

        def start(self, p):
            pl.when(z == self.last)(lambda: self.leave(p).start())
            pl.when(z != self.last)(lambda: self.direct(p).start())

        def relay(self, p):
            @pl.when(z == (self.receiver if p >= SPLIT else self.last))
            def _():
                self.leave(p).wait_recv()
                self.onward(p).start()

        def arrive(self, p):
            if p >= SPLIT:
                pl.when(z == self.receiver)(lambda: self.onward(p).wait_recv())
                pl.when(z != self.receiver)(lambda: self.direct(p).wait_recv())
            else:
                self.direct(p).wait_recv()

        def sent(self, p):
            self.direct(p).wait_send()
            if p >= SPLIT:
                pl.when(z == self.receiver)(lambda: self.onward(p).wait_send())
            else:
                pl.when(z == self.last)(lambda: self.leave(p).wait_send())

    rising = Side(1, 3, 1, low, via_up, HALO_UP, HOP_UP)
    falling = Side(0, 0, 3, high, via_down, HALO_DOWN, HOP_DOWN)

    def forward(p):
        rising.relay(p)
        falling.relay(p)

    for p in FIRST:
        rising.start(p)
        falling.start(p)

    for load in smalls:
        load.wait()
    row_dim = rows_s[0]
    col_dim = cols_s[0]
    loads[0].wait()

    @pl.loop(0, N // 128)
    def _(i):
        rows = pl.ds(pl.multiple_of(i * 128, 128), 128)
        row_id = lax.broadcasted_iota(jnp.int32, (128, N), 0) + i * 128
        col_id = lax.broadcasted_iota(jnp.int32, (128, N), 1)
        keep = (row_id < row_dim) & (col_id < col_dim)
        live[rows] = jnp.where(keep, live[rows].astype(F32), 0.0).astype(BF16)

    for load in loads[1:]:
        load.wait()

    gains = [coef_s[w] * on_s[w].astype(F32) for w in range(2)]

    chunks = range(CHUNKS)
    head, tail = pl.ds(0, 2), pl.ds(2, 2)
    relay_up = [remote(RELAY_UP + k, relay_out.at[0, k], relay_in.at[0, k], at_x(1)) for k in chunks]
    relay_down = [remote(RELAY_DOWN + k, relay_out.at[1, k], relay_in.at[1, k], at_x(3)) for k in chunks]
    up_b = [remote(UP_B + k, side_out.at[0, k, tail], from_left.at[k, tail], at_x(1)) for k in chunks]
    up_a = [remote(UP_A + k, side_out.at[0, k, head], from_left.at[k, head], at_x(1)) for k in chunks]
    down_a = [remote(DOWN_A + k, side_out.at[1, k, head], from_right.at[k, head], at_x(3)) for k in chunks]
    down_b = [remote(DOWN_B + k, side_out.at[1, k, tail], from_right.at[k, tail], at_x(3)) for k in chunks]

    def cols(k):
        return slice(k * WIDTH, (k + 1) * WIDTH)

    @pl.loop(0, 4)
    def _(i):
        owner = lax.rem(x + 2 + i, 4)
        rows = pl.ds(pl.multiple_of(owner * 192, 64), 192)
        total = None
        for w in range(2):
            applied = jnp.dot(left[w, rows, :], live[...], preferred_element_type=F32).astype(BF16)
            term = gains[w] * lax.dot_general(
                applied, right[w], (((1,), (1,)), ((), ())), preferred_element_type=F32
            )
            total = term if total is None else total + term
        acc[i] = total.reshape(4, BLK, N)

        @pl.when(i == 0)
        def _():
            for k in chunks:
                relay_out[0, k] = acc[0, 0:2, :, cols(k)].astype(BF16)
                relay_up[k].start()
                relay_out[1, k] = acc[0, 2:4, :, cols(k)].astype(BF16)
                relay_down[k].start()

        @pl.when(i == 1)
        def _():
            for k in chunks:
                side_out[1, k, 0:2] = acc[1, 0:2, :, cols(k)].astype(BF16)
                down_a[k].start()

        @pl.when(i == 3)
        def _():
            for k in chunks:
                side_out[0, k, 2:4] = acc[3, 2:4, :, cols(k)].astype(BF16)
                up_b[k].start()

    for k in chunks:
        relay_up[k].wait_recv()
        side_out[0, k, 0:2] = (acc[3, 0:2, :, cols(k)] + relay_in[0, k].astype(F32)).astype(BF16)
        up_a[k].start()
        relay_down[k].wait_recv()
        side_out[1, k, 2:4] = (acc[1, 2:4, :, cols(k)] + relay_in[1, k].astype(F32)).astype(BF16)
        down_b[k].start()

    def row_sum(k, j):
        return acc[2, j, :, cols(k)] + from_left[k, j].astype(F32) + from_right[k, j].astype(F32)

    def rs_z(k, d):
        return remote(RS_Z + 3 * k + d - 1, z_out.at[k, d - 1], z_in.at[k, d - 1], at_z(d))

    def sum_over_x(k):
        for copy in (up_b[k], down_a[k], up_a[k], down_b[k]):
            copy.wait_recv()
        for d in (2, 1, 3):
            z_out[k, d - 1] = row_sum(k, lax.rem(z + d, 4)).astype(BF16)
            rs_z(k, d).start()

    def own_block(k, d):
        return unit.at[k, x * 4 + lax.rem(z + 4 - d, 4)]

    def ag_z(k, d, shift):
        return remote(AG_Z + 3 * k + d - 1, own_block(k, shift), own_block(k, shift), at_z(d))

    def sum_over_z(k):
        mine = row_sum(k, z)
        for d in (1, 3, 2):
            rs_z(k, d).wait_recv()
            mine = mine + z_in[k, d - 1].astype(F32)
        row_id = lax.broadcasted_iota(jnp.int32, (BLK, WIDTH), 0) + bond * BLK
        col_id = lax.broadcasted_iota(jnp.int32, (BLK, WIDTH), 1) + k * WIDTH
        mine = jnp.where((row_id < row_dim) & (col_id < col_dim), mine, 0.0)
        rounded = mine.astype(BF16)
        unit[k, bond] = rounded
        matvec_o[:, cols(k)] = rounded
        for d in (2, 1, 3):
            ag_z(k, d, 0).start()
        square = mine * mine
        return sum(
            square[a : a + 8, b : b + 128] for a in range(0, BLK, 8) for b in range(0, WIDTH, 128)
        )

    def blocks(k, d, first, count):
        return unit.at[k, pl.ds(lax.rem(x + d, 4) * 4 + first, count)]

    def ag_up(k, d):
        return remote(AG_UP + k, blocks(k, d, 0, 4), blocks(k, d, 0, 4), at_x(1))

    def ag_down(k, d):
        return remote(AG_DOWN + k, blocks(k, d, 0, 4), blocks(k, d, 0, 4), at_x(3))

    def fwd_up(k, d):
        return remote(FWD_UP + k, blocks(k, d, 0, 2), blocks(k, d, 0, 2), at_x(1))

    def fwd_down(k, d):
        return remote(FWD_DOWN + k, blocks(k, d, 2, 2), blocks(k, d, 2, 2), at_x(3))

    def gather_z(k):
        for d in (1, 3, 2):
            ag_z(k, d, d).wait_recv()
        ag_up(k, 0).start()
        ag_down(k, 0).start()

    def gather_x(k):
        ag_up(k, 3).wait_recv()
        fwd_up(k, 3).start()
        ag_down(k, 1).wait_recv()
        fwd_down(k, 1).start()

    for k in chunks:
        sum_over_x(k)

    for p in SECOND:
        pl.when(z == 3)(lambda: rising.leave(p).start())
        pl.when(z == 0)(lambda: falling.leave(p).start())
    for p in (3, 4, 0):
        forward(p)

    def spread(i, stage, devices):
        return [
            remote(i + n, part.at[stage], part_in.at[i - SUM_Z + n], device) for n, device in enumerate(devices)
        ]

    sums = [
        spread(SUM_Z, 0, [at_z(1), at_z(2), at_z(3)]),
        spread(SUM_X, 1, [at_x(1), at_x(2), at_x(3)]),
        spread(SUM_S, 2, sectors),
    ]
    starts = [0, 3, 6, 13]

    def sum_start(stage, value):
        part[stage] = value
        for copy in sums[stage]:
            copy.start()

    def sum_finish(stage):
        for copy in sums[stage]:
            copy.wait_recv()
        return sum((part_in[n] for n in range(starts[stage], starts[stage + 1])), part[stage])

    sum_start(0, sum_over_z(0) + sum_over_z(1) + sum_over_z(2))
    for p in SECOND:
        pl.when(z != 3)(lambda: rising.direct(p).start())
        pl.when(z != 0)(lambda: falling.direct(p).start())

    forward(1)
    gather_z(0)
    gather_z(1)
    gather_z(2)
    sum_start(1, sum_finish(0))

    w_gain = [[table_s[index_s[w, k]] for k in range(3)] for w in range(2)]
    low_gain = jnp.where(bond > 0, w_gain[0][0], 0.0)
    high_gain = jnp.where(bond < 15, w_gain[1][2], 0.0)

    def mix(p):
        rows = rows_of(p)
        rising.arrive(p)
        falling.arrive(p)
        here = left[0, rows].astype(F32)
        there = left[1, rows].astype(F32)
        mixed[0, rows] = (low_gain * low[rows].astype(F32) + w_gain[0][1] * here + w_gain[0][2] * there).astype(BF16)
        mixed[1, rows] = (w_gain[1][0] * here + w_gain[1][1] * there + high_gain * high[rows].astype(F32)).astype(BF16)

    gather_x(0)
    gather_x(1)
    gather_x(2)
    forward(2)
    forward(5)
    sum_start(2, sum_finish(1))
    for p in (3, 0, 4, 1, 2):
        mix(p)

    stores = []

    def product(k, first, count, n):
        rows = pl.ds(first, count)
        for w in range(2):
            result = jnp.dot(mixed[w, rows, :], unit[k].reshape(N, WIDTH), preferred_element_type=F32)
            half[w, rows, cols(k)] = (result * LIFT).astype(BF16)
        area = half.at[:, rows, pl.ds(k * WIDTH, WIDTH)]
        stores.append(pltpu.make_async_copy(area, half_o.at[:, rows, pl.ds(k * WIDTH, WIDTH)], store_sem.at[n]))
        stores[-1].start()

    for k in chunks:
        fwd_up(k, 2).wait_recv()
        fwd_down(k, 2).wait_recv()
        product(k, 0, N - LAST, k)
        turned[cols(k)] = unit[k].reshape(N, WIDTH).T
        stores.append(pltpu.make_async_copy(turned.at[pl.ds(k * WIDTH, WIDTH)], turned_o.at[pl.ds(k * WIDTH, WIDTH)], store_sem.at[CHUNKS + k]))
        stores[-1].start()
    square_o[...] = sum_finish(2)
    mix(PIECES - 1)
    for k in chunks:
        product(k, N - LAST, LAST, 2 * CHUNKS + k)

    for k in chunks:
        for copy in (relay_up[k], relay_down[k], up_a[k], up_b[k], down_a[k], down_b[k]):
            copy.wait_send()
        for d in (1, 2, 3):
            rs_z(k, d).wait_send()
            ag_z(k, d, 0).wait_send()
        for copy in (ag_up(k, 0), ag_down(k, 0), fwd_up(k, 3), fwd_down(k, 1)):
            copy.wait_send()
    for stage in sums:
        for copy in stage:
            copy.wait_send()
    for p in range(PIECES):
        rising.sent(p)
        falling.sent(p)
    for store in stores:
        store.wait()


def last_product(matvec_h, half_h, turned_h, square_h, matvec_o, env_o, matvec, half, turned, square, grown, sem):
    loads = [
        pltpu.make_async_copy(turned_h, turned, sem.at[0]),
        pltpu.make_async_copy(half_h.at[0], half.at[0], sem.at[1]),
        pltpu.make_async_copy(half_h.at[1], half.at[1], sem.at[2]),
        pltpu.make_async_copy(square_h, square, sem.at[3]),
        pltpu.make_async_copy(matvec_h, matvec, sem.at[4]),
    ]
    for load in loads:
        load.start()
    loads[3].wait()
    scale = lax.rsqrt(jnp.full((1, N), jnp.sum(square[...]) * (1.0 / (8 * N * N)) + 1e-06, F32))
    loads[4].wait()
    stores = [pltpu.make_async_copy(matvec, matvec_o, sem.at[5])]
    stores[0].start()
    loads[0].wait()
    for w in range(2):
        loads[1 + w].wait()
        for k in range(N // TILE):
            rows = pl.ds(k * TILE, TILE)
            product = jnp.dot(turned[rows], half[w], preferred_element_type=F32)
            grown[w, rows] = (product * scale * (scale * (1.0 / (LIFT * math.sqrt(N))))).astype(BF16)
            stores.append(pltpu.make_async_copy(grown.at[w, rows], env_o.at[w, 0, rows], sem.at[6 + 3 * w + k]))
            stores[-1].start()
    for store in stores:
        store.wait()


def on_device(
    theta, sector_dims, right_dims, env_left, env_right, mpo_on, mpo_coef, mix_index, weight_table
):
    hbm = pl.BlockSpec(memory_space=pl.ANY)
    vmem = pl.BlockSpec(memory_space=pltpu.VMEM)
    matvec, half, turned, square = pl.pallas_call(
        body,
        out_shape=(
            jax.ShapeDtypeStruct((BLK, N), BF16),
            jax.ShapeDtypeStruct((2, N, N), BF16),
            jax.ShapeDtypeStruct((N, N), BF16),
            jax.ShapeDtypeStruct((8, 128), F32),
        ),
        in_specs=[hbm] * 9,
        out_specs=(vmem, hbm, hbm, vmem),
        scratch_shapes=[
            pltpu.SMEM((1,), jnp.int32),
            pltpu.SMEM((1,), jnp.int32),
            pltpu.SMEM((2,), jnp.int32),
            pltpu.SMEM((2,), F32),
            pltpu.SMEM((2, 3), jnp.int32),
            pltpu.SMEM((8,), F32),
            pltpu.VMEM((N, N), BF16),
            pltpu.VMEM((2, N, N), BF16),
            pltpu.VMEM((2, N, N), BF16),
            pltpu.VMEM((N, N), BF16),
            pltpu.VMEM((N, N), BF16),
            pltpu.VMEM((PIECES, max(SIZES), N), BF16),
            pltpu.VMEM((PIECES, max(SIZES), N), BF16),
            pltpu.VMEM((4, 4, BLK, N), F32),
            pltpu.VMEM((2, CHUNKS, 2, BLK, WIDTH), BF16),
            pltpu.VMEM((2, CHUNKS, 2, BLK, WIDTH), BF16),
            pltpu.VMEM((2, CHUNKS, 4, BLK, WIDTH), BF16),
            pltpu.VMEM((CHUNKS, 4, BLK, WIDTH), BF16),
            pltpu.VMEM((CHUNKS, 4, BLK, WIDTH), BF16),
            pltpu.VMEM((CHUNKS, 3, BLK, WIDTH), BF16),
            pltpu.VMEM((CHUNKS, 3, BLK, WIDTH), BF16),
            pltpu.VMEM((CHUNKS, 16, BLK, WIDTH), BF16),
            pltpu.VMEM((N, N), BF16),
            pltpu.VMEM((3, 8, 128), F32),
            pltpu.VMEM((13, 8, 128), F32),
            pltpu.VMEM((2, N, N), BF16),
            pltpu.VMEM((2, N, N), BF16),
            pltpu.SemaphoreType.DMA((6,)),
            pltpu.SemaphoreType.DMA((5,)),
            pltpu.SemaphoreType.DMA((COPIES,)),
            pltpu.SemaphoreType.DMA((COPIES,)),
            pltpu.SemaphoreType.DMA((3 * CHUNKS,)),
        ],
        compiler_params=pltpu.CompilerParams(
            collective_id=0, has_side_effects=True, vmem_limit_bytes=56 * 1024 * 1024
        ),
        name="sweep",
    )(theta, env_left, env_right, sector_dims, right_dims, mpo_on, mpo_coef, mix_index, weight_table)
    matvec, env_next = pl.pallas_call(
        last_product,
        out_shape=(jax.ShapeDtypeStruct((BLK, N), BF16), jax.ShapeDtypeStruct(env_left.shape, BF16)),
        in_specs=[hbm] * 4,
        out_specs=(hbm, hbm),
        scratch_shapes=[
            pltpu.VMEM((BLK, N), BF16),
            pltpu.VMEM((2, N, N), BF16),
            pltpu.VMEM((N, N), BF16),
            pltpu.VMEM((8, 128), F32),
            pltpu.VMEM((2, N, N), BF16),
            pltpu.SemaphoreType.DMA((12,)),
        ],
        compiler_params=pltpu.CompilerParams(vmem_limit_bytes=56 * 1024 * 1024),
        name="last_product",
    )(matvec, half, turned, square)
    return (matvec[None], env_next)


def solution(mesh):
    split = Mesh(mesh.devices.reshape(4, 4, 4, 2), AXES)
    in_specs = (
        P(SECTOR, None, None),
        P(SECTOR),
        P(SECTOR),
        P(BOND, SECTOR, None, None),
        P(BOND, SECTOR, None, None),
        P(BOND),
        P(BOND),
        P(BOND, None),
        P(),
    )
    out_specs = (P(SECTOR, BOND, None), P(BOND, SECTOR, None, None))
    return jax.shard_map(on_device, mesh=split, in_specs=in_specs, out_specs=out_specs, check_vma=False)
```

```python
import math

import jax
import jax.numpy as jnp
from jax import lax
from jax.experimental import pallas as pl
from jax.experimental.pallas import tpu as pltpu
from jax.sharding import Mesh
from jax.sharding import PartitionSpec as P

AXES = ("bond_0", "bond_1", "sector_0", "sector_1")
BOND = ("bond_0", "bond_1")
SECTOR = ("sector_0", "sector_1")
MESH = pl.DeviceIdType.MESH
F32 = jnp.float32
BF16 = jnp.bfloat16

N = 768
BLK = 48
SIZES = (96, 128, 96, 160, 160, 128)
PIECES = len(SIZES)
LAST = SIZES[-1]
SPLIT = 3
FIRST = (3, 4, 5, 0)
SECOND = (1, 2)
LIFT = 1024.0
TILE = 256

CHUNKS = 3
WIDTH = N // CHUNKS

RELAY_UP, RELAY_DOWN, UP_B, DOWN_A, UP_A, DOWN_B = range(0, 6 * CHUNKS, CHUNKS)
RS_Z = 6 * CHUNKS
AG_Z = 9 * CHUNKS
AG_UP, AG_DOWN, FWD_UP, FWD_DOWN = range(12 * CHUNKS, 16 * CHUNKS, CHUNKS)
SUM_Z = 16 * CHUNKS
SUM_X = SUM_Z + 3
SUM_S = SUM_X + 3
HALO_UP = SUM_S + 7
HALO_DOWN = HALO_UP + PIECES
HOP_UP = HALO_DOWN + PIECES
HOP_DOWN = HOP_UP + PIECES
COPIES = HOP_DOWN + PIECES


def body(
    theta_h, left_h, right_h, rows_h, cols_h, on_h, coef_h, index_h, table_h,
    matvec_o, env_o,
    rows_s, cols_s, on_s, coef_s, index_s, table_s,
    live, left, right, low, high, via_up, via_down, acc, relay_out, relay_in, side_out, from_left, from_right,
    z_out, z_in, unit, turned, part, part_in, mixed, half, grown_sum, grown,
    small_sem, load_sem, send_sem, recv_sem, store_sem,
):
    x = lax.axis_index("bond_0")
    z = lax.axis_index("bond_1")
    y = lax.axis_index("sector_0")
    c = lax.axis_index("sector_1")

    def at_x(d):
        return {"bond_0": lax.rem(x + d, 4)}

    def at_z(d):
        return {"bond_1": lax.rem(z + d, 4)}

    def at_y(d):
        return {"sector_0": lax.rem(y + d, 4)}

    other = {"sector_1": 1 - c}
    bond = x * 4 + z
    sectors = [other] + [at_y(d) for d in (1, 2, 3)] + [{**at_y(d), **other} for d in (1, 2, 3)]
    peers = [at_x(1), at_x(2), at_x(3), at_z(1), at_z(2), at_z(3)] + sectors

    def remote(i, src, dst, device):
        return pltpu.make_async_remote_copy(
            src_ref=src, dst_ref=dst, send_sem=send_sem.at[i], recv_sem=recv_sem.at[i],
            device_id=device, device_id_type=MESH,
        )

    loads = [
        pltpu.make_async_copy(theta_h.at[0], live, load_sem.at[0]),
        pltpu.make_async_copy(left_h.at[0, 0], left.at[0], load_sem.at[1]),
        pltpu.make_async_copy(left_h.at[1, 0], left.at[1], load_sem.at[2]),
        pltpu.make_async_copy(right_h.at[0, 0], right.at[0], load_sem.at[3]),
        pltpu.make_async_copy(right_h.at[1, 0], right.at[1], load_sem.at[4]),
    ]
    smalls = [
        pltpu.make_async_copy(source, target, small_sem.at[n])
        for n, (source, target) in enumerate(
            [(rows_h, rows_s), (cols_h, cols_s), (on_h, on_s), (coef_h, coef_s), (index_h, index_s), (table_h, table_s)]
        )
    ]
    barrier = pltpu.get_barrier_semaphore()
    for peer in peers:
        pl.semaphore_signal(barrier, inc=1, device_id=peer, device_id_type=MESH)
    for load in smalls + loads:
        load.start()
    pl.semaphore_wait(barrier, len(peers))

    def rows_of(p):
        return pl.ds(sum(SIZES[:p]), SIZES[p])

    class Side:
        def __init__(self, channel, last, step, target, via, first, hop):
            self.channel, self.last, self.step, self.target, self.via = channel, last, step, target, via
            self.first_sem, self.hop_sem, self.receiver = first, hop, 3 - last

        def stop(self, p):
            return self.via.at[p, pl.ds(0, SIZES[p])]

        def source(self, p):
            return left_h.at[self.channel, 0, rows_of(p)]

        def along_z(self, p, source, target):
            return remote(self.first_sem + p, source, target, at_z(self.step))

        def along_x(self, p, source, target):
            return remote(self.hop_sem + p, source, target, at_x(self.step))

        def direct(self, p):
            return self.along_z(p, self.source(p), self.target.at[rows_of(p)])

        def leave(self, p):
            if p >= SPLIT:
                return self.along_z(p, self.source(p), self.stop(p))
            return self.along_x(p, self.source(p), self.stop(p))

        def onward(self, p):
            if p >= SPLIT:
                return self.along_x(p, self.stop(p), self.target.at[rows_of(p)])
            return self.along_z(p, self.stop(p), self.target.at[rows_of(p)])

        def start(self, p):
            pl.when(z == self.last)(lambda: self.leave(p).start())
            pl.when(z != self.last)(lambda: self.direct(p).start())

        def relay(self, p):
            @pl.when(z == (self.receiver if p >= SPLIT else self.last))
            def _():
                self.leave(p).wait_recv()
                self.onward(p).start()

        def arrive(self, p):
            if p >= SPLIT:
                pl.when(z == self.receiver)(lambda: self.onward(p).wait_recv())
                pl.when(z != self.receiver)(lambda: self.direct(p).wait_recv())
            else:
                self.direct(p).wait_recv()

        def sent(self, p):
            self.direct(p).wait_send()
            if p >= SPLIT:
                pl.when(z == self.receiver)(lambda: self.onward(p).wait_send())
            else:
                pl.when(z == self.last)(lambda: self.leave(p).wait_send())

    rising = Side(1, 3, 1, low, via_up, HALO_UP, HOP_UP)
    falling = Side(0, 0, 3, high, via_down, HALO_DOWN, HOP_DOWN)

    def forward(p):
        rising.relay(p)
        falling.relay(p)

    for p in FIRST:
        rising.start(p)
        falling.start(p)

    for load in smalls:
        load.wait()
    row_dim = rows_s[0]
    col_dim = cols_s[0]
    loads[0].wait()

    @pl.loop(0, N // 128)
    def _(i):
        rows = pl.ds(pl.multiple_of(i * 128, 128), 128)
        row_id = lax.broadcasted_iota(jnp.int32, (128, N), 0) + i * 128
        col_id = lax.broadcasted_iota(jnp.int32, (128, N), 1)
        keep = (row_id < row_dim) & (col_id < col_dim)
        live[rows] = jnp.where(keep, live[rows].astype(F32), 0.0).astype(BF16)

    for load in loads[1:]:
        load.wait()

    gains = [coef_s[w] * on_s[w].astype(F32) for w in range(2)]

    chunks = range(CHUNKS)
    head, tail = pl.ds(0, 2), pl.ds(2, 2)
    relay_up = [remote(RELAY_UP + k, relay_out.at[0, k], relay_in.at[0, k], at_x(1)) for k in chunks]
    relay_down = [remote(RELAY_DOWN + k, relay_out.at[1, k], relay_in.at[1, k], at_x(3)) for k in chunks]
    up_b = [remote(UP_B + k, side_out.at[0, k, tail], from_left.at[k, tail], at_x(1)) for k in chunks]
    up_a = [remote(UP_A + k, side_out.at[0, k, head], from_left.at[k, head], at_x(1)) for k in chunks]
    down_a = [remote(DOWN_A + k, side_out.at[1, k, head], from_right.at[k, head], at_x(3)) for k in chunks]
    down_b = [remote(DOWN_B + k, side_out.at[1, k, tail], from_right.at[k, tail], at_x(3)) for k in chunks]

    def cols(k):
        return slice(k * WIDTH, (k + 1) * WIDTH)

    @pl.loop(0, 4)
    def _(i):
        owner = lax.rem(x + 2 + i, 4)
        rows = pl.ds(pl.multiple_of(owner * 192, 64), 192)
        total = None
        for w in range(2):
            applied = jnp.dot(left[w, rows, :], live[...], preferred_element_type=F32).astype(BF16)
            term = gains[w] * lax.dot_general(
                applied, right[w], (((1,), (1,)), ((), ())), preferred_element_type=F32
            )
            total = term if total is None else total + term
        acc[i] = total.reshape(4, BLK, N)

        @pl.when(i == 0)
        def _():
            for k in chunks:
                relay_out[0, k] = acc[0, 0:2, :, cols(k)].astype(BF16)
                relay_up[k].start()
                relay_out[1, k] = acc[0, 2:4, :, cols(k)].astype(BF16)
                relay_down[k].start()

        @pl.when(i == 1)
        def _():
            for k in chunks:
                side_out[1, k, 0:2] = acc[1, 0:2, :, cols(k)].astype(BF16)
                down_a[k].start()

        @pl.when(i == 3)
        def _():
            for k in chunks:
                side_out[0, k, 2:4] = acc[3, 2:4, :, cols(k)].astype(BF16)
                up_b[k].start()

    for k in chunks:
        relay_up[k].wait_recv()
        side_out[0, k, 0:2] = (acc[3, 0:2, :, cols(k)] + relay_in[0, k].astype(F32)).astype(BF16)
        up_a[k].start()
        relay_down[k].wait_recv()
        side_out[1, k, 2:4] = (acc[1, 2:4, :, cols(k)] + relay_in[1, k].astype(F32)).astype(BF16)
        down_b[k].start()

    def row_sum(k, j):
        return acc[2, j, :, cols(k)] + from_left[k, j].astype(F32) + from_right[k, j].astype(F32)

    def rs_z(k, d):
        return remote(RS_Z + 3 * k + d - 1, z_out.at[k, d - 1], z_in.at[k, d - 1], at_z(d))

    def sum_over_x(k):
        for copy in (up_b[k], down_a[k], up_a[k], down_b[k]):
            copy.wait_recv()
        for d in (2, 1, 3):
            z_out[k, d - 1] = row_sum(k, lax.rem(z + d, 4)).astype(BF16)
            rs_z(k, d).start()

    def own_block(k, d):
        return unit.at[k, x * 4 + lax.rem(z + 4 - d, 4)]

    def ag_z(k, d, shift):
        return remote(AG_Z + 3 * k + d - 1, own_block(k, shift), own_block(k, shift), at_z(d))

    def sum_over_z(k):
        mine = row_sum(k, z)
        for d in (1, 3, 2):
            rs_z(k, d).wait_recv()
            mine = mine + z_in[k, d - 1].astype(F32)
        row_id = lax.broadcasted_iota(jnp.int32, (BLK, WIDTH), 0) + bond * BLK
        col_id = lax.broadcasted_iota(jnp.int32, (BLK, WIDTH), 1) + k * WIDTH
        mine = jnp.where((row_id < row_dim) & (col_id < col_dim), mine, 0.0)
        rounded = mine.astype(BF16)
        unit[k, bond] = rounded
        matvec_o[:, cols(k)] = rounded
        for d in (2, 1, 3):
            ag_z(k, d, 0).start()
        square = mine * mine
        return sum(
            square[a : a + 8, b : b + 128] for a in range(0, BLK, 8) for b in range(0, WIDTH, 128)
        )

    def blocks(k, d, first, count):
        return unit.at[k, pl.ds(lax.rem(x + d, 4) * 4 + first, count)]

    def ag_up(k, d):
        return remote(AG_UP + k, blocks(k, d, 0, 4), blocks(k, d, 0, 4), at_x(1))

    def ag_down(k, d):
        return remote(AG_DOWN + k, blocks(k, d, 0, 4), blocks(k, d, 0, 4), at_x(3))

    def fwd_up(k, d):
        return remote(FWD_UP + k, blocks(k, d, 0, 2), blocks(k, d, 0, 2), at_x(1))

    def fwd_down(k, d):
        return remote(FWD_DOWN + k, blocks(k, d, 2, 2), blocks(k, d, 2, 2), at_x(3))

    def gather_z(k):
        for d in (1, 3, 2):
            ag_z(k, d, d).wait_recv()
        ag_up(k, 0).start()
        ag_down(k, 0).start()

    def gather_x(k):
        ag_up(k, 3).wait_recv()
        fwd_up(k, 3).start()
        ag_down(k, 1).wait_recv()
        fwd_down(k, 1).start()

    for k in chunks:
        sum_over_x(k)

    for p in SECOND:
        pl.when(z == 3)(lambda: rising.leave(p).start())
        pl.when(z == 0)(lambda: falling.leave(p).start())
    for p in (3, 4, 0):
        forward(p)

    def spread(i, stage, devices):
        return [
            remote(i + n, part.at[stage], part_in.at[i - SUM_Z + n], device) for n, device in enumerate(devices)
        ]

    sums = [
        spread(SUM_Z, 0, [at_z(1), at_z(2), at_z(3)]),
        spread(SUM_X, 1, [at_x(1), at_x(2), at_x(3)]),
        spread(SUM_S, 2, sectors),
    ]
    starts = [0, 3, 6, 13]

    def sum_start(stage, value):
        part[stage] = value
        for copy in sums[stage]:
            copy.start()

    def sum_finish(stage):
        for copy in sums[stage]:
            copy.wait_recv()
        return sum((part_in[n] for n in range(starts[stage], starts[stage + 1])), part[stage])

    sum_start(0, sum_over_z(0) + sum_over_z(1) + sum_over_z(2))
    for p in SECOND:
        pl.when(z != 3)(lambda: rising.direct(p).start())
        pl.when(z != 0)(lambda: falling.direct(p).start())

    forward(1)
    gather_z(0)
    gather_z(1)
    gather_z(2)
    sum_start(1, sum_finish(0))

    w_gain = [[table_s[index_s[w, k]] for k in range(3)] for w in range(2)]
    low_gain = jnp.where(bond > 0, w_gain[0][0], 0.0)
    high_gain = jnp.where(bond < 15, w_gain[1][2], 0.0)

    def mix(p):
        rows = rows_of(p)
        rising.arrive(p)
        falling.arrive(p)
        here = left[0, rows].astype(F32)
        there = left[1, rows].astype(F32)
        mixed[0, rows] = (low_gain * low[rows].astype(F32) + w_gain[0][1] * here + w_gain[0][2] * there).astype(BF16)
        mixed[1, rows] = (w_gain[1][0] * here + w_gain[1][1] * there + high_gain * high[rows].astype(F32)).astype(BF16)

    gather_x(0)
    gather_x(1)
    forward(2)
    gather_x(2)
    forward(5)
    sum_start(2, sum_finish(1))
    for p in (3, 0, 4, 1, 2):
        mix(p)

    def product(k, first, count):
        rows = pl.ds(first, count)
        for w in range(2):
            result = jnp.dot(mixed[w, rows, :], unit[k].reshape(N, WIDTH), preferred_element_type=F32)
            half[w, rows, cols(k)] = (result * LIFT).astype(BF16)

    for k in chunks:
        fwd_up(k, 2).wait_recv()
        fwd_down(k, 2).wait_recv()
        product(k, 0, N - LAST)
        turned[cols(k)] = unit[k].reshape(N, WIDTH).T
    for w in range(2):
        for k in range(N // TILE):
            rows = slice(k * TILE, (k + 1) * TILE)
            grown_sum[w, rows] = jnp.dot(
                turned[rows, : N - LAST], half[w, : N - LAST, :], preferred_element_type=F32
            )
    square_total = jnp.sum(sum_finish(2))
    scale = lax.rsqrt(jnp.full((1, N), square_total * (1.0 / (8 * N * N)) + 1e-06, F32))
    mix(PIECES - 1)
    for k in chunks:
        product(k, N - LAST, LAST)
    stores = []
    for w in range(2):
        for k in range(N // TILE):
            rows = pl.ds(k * TILE, TILE)
            result = grown_sum[w, rows] + jnp.dot(
                turned[rows, N - LAST :], half[w, N - LAST :, :], preferred_element_type=F32
            )
            grown[w, rows] = (result * scale * (scale * (1.0 / (LIFT * math.sqrt(N))))).astype(BF16)
            stores.append(pltpu.make_async_copy(grown.at[w, rows], env_o.at[w, 0, rows], store_sem.at[3 * w + k]))
            stores[-1].start()

    for k in chunks:
        for copy in (relay_up[k], relay_down[k], up_a[k], up_b[k], down_a[k], down_b[k]):
            copy.wait_send()
        for d in (1, 2, 3):
            rs_z(k, d).wait_send()
            ag_z(k, d, 0).wait_send()
        for copy in (ag_up(k, 0), ag_down(k, 0), fwd_up(k, 3), fwd_down(k, 1)):
            copy.wait_send()
    for stage in sums:
        for copy in stage:
            copy.wait_send()
    for p in range(PIECES):
        rising.sent(p)
        falling.sent(p)
    for store in stores:
        store.wait()


def hand_on(matvec_h, env_h, matvec_o, env_o, matvec, env, load_sem, store_sem):
    loads = [pltpu.make_async_copy(matvec_h, matvec, load_sem.at[0])]
    stores = [pltpu.make_async_copy(matvec, matvec_o, store_sem.at[0])]
    for w in range(2):
        for k in range(N // TILE):
            n = 3 * w + k
            rows = pl.ds(k * TILE, TILE)
            loads.append(pltpu.make_async_copy(env_h.at[w, 0, rows], env.at[n], load_sem.at[n + 1]))
            stores.append(pltpu.make_async_copy(env.at[n], env_o.at[w, 0, rows], store_sem.at[n + 1]))
    for load in loads:
        load.start()
    for load, store in zip(loads, stores):
        load.wait()
        store.start()
    for store in stores:
        store.wait()


def on_device(
    theta, sector_dims, right_dims, env_left, env_right, mpo_on, mpo_coef, mix_index, weight_table
):
    hbm = pl.BlockSpec(memory_space=pl.ANY)
    vmem = pl.BlockSpec(memory_space=pltpu.VMEM)
    matvec, env_next = pl.pallas_call(
        body,
        out_shape=(
            jax.ShapeDtypeStruct((BLK, N), BF16),
            jax.ShapeDtypeStruct(env_left.shape, BF16),
        ),
        in_specs=[hbm] * 9,
        out_specs=(vmem, hbm),
        scratch_shapes=[
            pltpu.SMEM((1,), jnp.int32),
            pltpu.SMEM((1,), jnp.int32),
            pltpu.SMEM((2,), jnp.int32),
            pltpu.SMEM((2,), F32),
            pltpu.SMEM((2, 3), jnp.int32),
            pltpu.SMEM((8,), F32),
            pltpu.VMEM((N, N), BF16),
            pltpu.VMEM((2, N, N), BF16),
            pltpu.VMEM((2, N, N), BF16),
            pltpu.VMEM((N, N), BF16),
            pltpu.VMEM((N, N), BF16),
            pltpu.VMEM((PIECES, max(SIZES), N), BF16),
            pltpu.VMEM((PIECES, max(SIZES), N), BF16),
            pltpu.VMEM((4, 4, BLK, N), F32),
            pltpu.VMEM((2, CHUNKS, 2, BLK, WIDTH), BF16),
            pltpu.VMEM((2, CHUNKS, 2, BLK, WIDTH), BF16),
            pltpu.VMEM((2, CHUNKS, 4, BLK, WIDTH), BF16),
            pltpu.VMEM((CHUNKS, 4, BLK, WIDTH), BF16),
            pltpu.VMEM((CHUNKS, 4, BLK, WIDTH), BF16),
            pltpu.VMEM((CHUNKS, 3, BLK, WIDTH), BF16),
            pltpu.VMEM((CHUNKS, 3, BLK, WIDTH), BF16),
            pltpu.VMEM((CHUNKS, 16, BLK, WIDTH), BF16),
            pltpu.VMEM((N, N), BF16),
            pltpu.VMEM((3, 8, 128), F32),
            pltpu.VMEM((13, 8, 128), F32),
            pltpu.VMEM((2, N, N), BF16),
            pltpu.VMEM((2, N, N), BF16),
            pltpu.VMEM((2, N, N), F32),
            pltpu.VMEM((2, N, N), BF16),
            pltpu.SemaphoreType.DMA((6,)),
            pltpu.SemaphoreType.DMA((5,)),
            pltpu.SemaphoreType.DMA((COPIES,)),
            pltpu.SemaphoreType.DMA((COPIES,)),
            pltpu.SemaphoreType.DMA((6,)),
        ],
        compiler_params=pltpu.CompilerParams(
            collective_id=0, has_side_effects=True, vmem_limit_bytes=56 * 1024 * 1024
        ),
        name="sweep",
    )(theta, env_left, env_right, sector_dims, right_dims, mpo_on, mpo_coef, mix_index, weight_table)
    matvec, env_next = pl.pallas_call(
        hand_on,
        out_shape=(jax.ShapeDtypeStruct((BLK, N), BF16), jax.ShapeDtypeStruct(env_left.shape, BF16)),
        in_specs=[hbm, hbm],
        out_specs=(hbm, hbm),
        scratch_shapes=[
            pltpu.VMEM((BLK, N), BF16),
            pltpu.VMEM((6, TILE, N), BF16),
            pltpu.SemaphoreType.DMA((7,)),
            pltpu.SemaphoreType.DMA((7,)),
        ],
        compiler_params=pltpu.CompilerParams(vmem_limit_bytes=56 * 1024 * 1024),
        name="hand_on",
    )(matvec, env_next)
    return (matvec[None], env_next)


def solution(mesh):
    split = Mesh(mesh.devices.reshape(4, 4, 4, 2), AXES)
    in_specs = (
        P(SECTOR, None, None),
        P(SECTOR),
        P(SECTOR),
        P(BOND, SECTOR, None, None),
        P(BOND, SECTOR, None, None),
        P(BOND),
        P(BOND),
        P(BOND, None),
        P(),
    )
    out_specs = (P(SECTOR, BOND, None), P(BOND, SECTOR, None, None))
    return jax.shard_map(on_device, mesh=split, in_specs=in_specs, out_specs=out_specs, check_vma=False)
```

```python
import math

import jax
import jax.numpy as jnp
from jax import lax
from jax.experimental import pallas as pl
from jax.experimental.pallas import tpu as pltpu
from jax.sharding import Mesh
from jax.sharding import PartitionSpec as P

AXES = ("bond_0", "bond_1", "sector_0", "sector_1")
BOND = ("bond_0", "bond_1")
SECTOR = ("sector_0", "sector_1")
MESH = pl.DeviceIdType.MESH
F32 = jnp.float32
BF16 = jnp.bfloat16

N = 768
BLK = 48
SIZES = (80, 112, 96, 176, 176, 128)
PIECES = len(SIZES)
LAST = SIZES[-1]
SPLIT = 3
FIRST = (3, 4, 0)
SECOND = (1, 2)
LIFT = 1024.0
TILE = 256

CHUNKS = 3
WIDTH = N // CHUNKS

RELAY_UP, RELAY_DOWN, UP_B, DOWN_A, UP_A, DOWN_B = range(0, 6 * CHUNKS, CHUNKS)
RS_Z = 6 * CHUNKS
AG_Z = 9 * CHUNKS
AG_UP, AG_DOWN, FWD_UP, FWD_DOWN = range(12 * CHUNKS, 16 * CHUNKS, CHUNKS)
SUM_Z = 16 * CHUNKS
SUM_X = SUM_Z + 3
SUM_S = SUM_X + 3
HALO_UP = SUM_S + 7
HALO_DOWN = HALO_UP + PIECES
HOP_UP = HALO_DOWN + PIECES
HOP_DOWN = HOP_UP + PIECES
COPIES = HOP_DOWN + PIECES


def body(
    theta_h, left_h, right_h, rows_h, cols_h, on_h, coef_h, index_h, table_h,
    matvec_o, env_o,
    rows_s, cols_s, on_s, coef_s, index_s, table_s,
    live, left, right, low, high, via_up, via_down, acc, relay_out, relay_in, side_out, from_left, from_right,
    z_out, z_in, unit, turned, part, part_in, mixed, half, grown_sum, grown,
    small_sem, load_sem, send_sem, recv_sem, store_sem,
):
    x = lax.axis_index("bond_0")
    z = lax.axis_index("bond_1")
    y = lax.axis_index("sector_0")
    c = lax.axis_index("sector_1")

    def at_x(d):
        return {"bond_0": lax.rem(x + d, 4)}

    def at_z(d):
        return {"bond_1": lax.rem(z + d, 4)}

    def at_y(d):
        return {"sector_0": lax.rem(y + d, 4)}

    other = {"sector_1": 1 - c}
    bond = x * 4 + z
    sectors = [other] + [at_y(d) for d in (1, 2, 3)] + [{**at_y(d), **other} for d in (1, 2, 3)]
    peers = [at_x(1), at_x(2), at_x(3), at_z(1), at_z(2), at_z(3)] + sectors

    def remote(i, src, dst, device):
        return pltpu.make_async_remote_copy(
            src_ref=src, dst_ref=dst, send_sem=send_sem.at[i], recv_sem=recv_sem.at[i],
            device_id=device, device_id_type=MESH,
        )

    loads = [
        pltpu.make_async_copy(theta_h.at[0], live, load_sem.at[0]),
        pltpu.make_async_copy(left_h.at[0, 0], left.at[0], load_sem.at[1]),
        pltpu.make_async_copy(left_h.at[1, 0], left.at[1], load_sem.at[2]),
        pltpu.make_async_copy(right_h.at[0, 0], right.at[0], load_sem.at[3]),
        pltpu.make_async_copy(right_h.at[1, 0], right.at[1], load_sem.at[4]),
    ]
    smalls = [
        pltpu.make_async_copy(source, target, small_sem.at[n])
        for n, (source, target) in enumerate(
            [(rows_h, rows_s), (cols_h, cols_s), (on_h, on_s), (coef_h, coef_s), (index_h, index_s), (table_h, table_s)]
        )
    ]
    barrier = pltpu.get_barrier_semaphore()
    for peer in peers:
        pl.semaphore_signal(barrier, inc=1, device_id=peer, device_id_type=MESH)
    for load in smalls + loads:
        load.start()
    pl.semaphore_wait(barrier, len(peers))

    def rows_of(p):
        return pl.ds(sum(SIZES[:p]), SIZES[p])

    class Side:
        def __init__(self, channel, last, step, target, via, first, hop):
            self.channel, self.last, self.step, self.target, self.via = channel, last, step, target, via
            self.first_sem, self.hop_sem, self.receiver = first, hop, 3 - last

        def stop(self, p):
            return self.via.at[p, pl.ds(0, SIZES[p])]

        def source(self, p):
            return left_h.at[self.channel, 0, rows_of(p)]

        def along_z(self, p, source, target):
            return remote(self.first_sem + p, source, target, at_z(self.step))

        def along_x(self, p, source, target):
            return remote(self.hop_sem + p, source, target, at_x(self.step))

        def direct(self, p):
            return self.along_z(p, self.source(p), self.target.at[rows_of(p)])

        def leave(self, p):
            if p >= SPLIT:
                return self.along_z(p, self.source(p), self.stop(p))
            return self.along_x(p, self.source(p), self.stop(p))

        def onward(self, p):
            if p >= SPLIT:
                return self.along_x(p, self.stop(p), self.target.at[rows_of(p)])
            return self.along_z(p, self.stop(p), self.target.at[rows_of(p)])

        def start(self, p):
            pl.when(z == self.last)(lambda: self.leave(p).start())
            pl.when(z != self.last)(lambda: self.direct(p).start())

        def relay(self, p):
            @pl.when(z == (self.receiver if p >= SPLIT else self.last))
            def _():
                self.leave(p).wait_recv()
                self.onward(p).start()

        def arrive(self, p):
            if p >= SPLIT:
                pl.when(z == self.receiver)(lambda: self.onward(p).wait_recv())
                pl.when(z != self.receiver)(lambda: self.direct(p).wait_recv())
            else:
                self.direct(p).wait_recv()

        def sent(self, p):
            self.direct(p).wait_send()
            if p >= SPLIT:
                pl.when(z == self.receiver)(lambda: self.onward(p).wait_send())
            else:
                pl.when(z == self.last)(lambda: self.leave(p).wait_send())

    rising = Side(1, 3, 1, low, via_up, HALO_UP, HOP_UP)
    falling = Side(0, 0, 3, high, via_down, HALO_DOWN, HOP_DOWN)

    def forward(p):
        rising.relay(p)
        falling.relay(p)

    for p in FIRST:
        rising.start(p)
        falling.start(p)

    for load in smalls:
        load.wait()
    row_dim = rows_s[0]
    col_dim = cols_s[0]
    loads[0].wait()

    @pl.loop(0, N // 128)
    def _(i):
        rows = pl.ds(pl.multiple_of(i * 128, 128), 128)
        row_id = lax.broadcasted_iota(jnp.int32, (128, N), 0) + i * 128
        col_id = lax.broadcasted_iota(jnp.int32, (128, N), 1)
        keep = (row_id < row_dim) & (col_id < col_dim)
        live[rows] = jnp.where(keep, live[rows].astype(F32), 0.0).astype(BF16)

    for load in loads[1:]:
        load.wait()

    gains = [coef_s[w] * on_s[w].astype(F32) for w in range(2)]

    chunks = range(CHUNKS)
    head, tail = pl.ds(0, 2), pl.ds(2, 2)
    relay_up = [remote(RELAY_UP + k, relay_out.at[0, k], relay_in.at[0, k], at_x(1)) for k in chunks]
    relay_down = [remote(RELAY_DOWN + k, relay_out.at[1, k], relay_in.at[1, k], at_x(3)) for k in chunks]
    up_b = [remote(UP_B + k, side_out.at[0, k, tail], from_left.at[k, tail], at_x(1)) for k in chunks]
    up_a = [remote(UP_A + k, side_out.at[0, k, head], from_left.at[k, head], at_x(1)) for k in chunks]
    down_a = [remote(DOWN_A + k, side_out.at[1, k, head], from_right.at[k, head], at_x(3)) for k in chunks]
    down_b = [remote(DOWN_B + k, side_out.at[1, k, tail], from_right.at[k, tail], at_x(3)) for k in chunks]

    def cols(k):
        return slice(k * WIDTH, (k + 1) * WIDTH)

    @pl.loop(0, 4)
    def _(i):
        owner = lax.rem(x + 2 + i, 4)
        rows = pl.ds(pl.multiple_of(owner * 192, 64), 192)
        total = None
        for w in range(2):
            applied = jnp.dot(left[w, rows, :], live[...], preferred_element_type=F32).astype(BF16)
            term = gains[w] * lax.dot_general(
                applied, right[w], (((1,), (1,)), ((), ())), preferred_element_type=F32
            )
            total = term if total is None else total + term
        acc[i] = total.reshape(4, BLK, N)

        @pl.when(i == 0)
        def _():
            for k in chunks:
                relay_out[0, k] = acc[0, 0:2, :, cols(k)].astype(BF16)
                relay_up[k].start()
                relay_out[1, k] = acc[0, 2:4, :, cols(k)].astype(BF16)
                relay_down[k].start()

        @pl.when(i == 1)
        def _():
            for k in chunks:
                side_out[1, k, 0:2] = acc[1, 0:2, :, cols(k)].astype(BF16)
                down_a[k].start()

        @pl.when(i == 3)
        def _():
            for k in chunks:
                side_out[0, k, 2:4] = acc[3, 2:4, :, cols(k)].astype(BF16)
                up_b[k].start()

    for k in chunks:
        relay_up[k].wait_recv()
        side_out[0, k, 0:2] = (acc[3, 0:2, :, cols(k)] + relay_in[0, k].astype(F32)).astype(BF16)
        up_a[k].start()
        relay_down[k].wait_recv()
        side_out[1, k, 2:4] = (acc[1, 2:4, :, cols(k)] + relay_in[1, k].astype(F32)).astype(BF16)
        down_b[k].start()

    def row_sum(k, j):
        return acc[2, j, :, cols(k)] + from_left[k, j].astype(F32) + from_right[k, j].astype(F32)

    def rs_z(k, d):
        return remote(RS_Z + 3 * k + d - 1, z_out.at[k, d - 1], z_in.at[k, d - 1], at_z(d))

    def sum_over_x(k):
        for copy in (up_b[k], down_a[k], up_a[k], down_b[k]):
            copy.wait_recv()
        for d in (2, 1, 3):
            z_out[k, d - 1] = row_sum(k, lax.rem(z + d, 4)).astype(BF16)
            rs_z(k, d).start()

    def own_block(k, d):
        return unit.at[k, x * 4 + lax.rem(z + 4 - d, 4)]

    def ag_z(k, d, shift):
        return remote(AG_Z + 3 * k + d - 1, own_block(k, shift), own_block(k, shift), at_z(d))

    def sum_over_z(k):
        mine = row_sum(k, z)
        for d in (1, 3, 2):
            rs_z(k, d).wait_recv()
            mine = mine + z_in[k, d - 1].astype(F32)
        row_id = lax.broadcasted_iota(jnp.int32, (BLK, WIDTH), 0) + bond * BLK
        col_id = lax.broadcasted_iota(jnp.int32, (BLK, WIDTH), 1) + k * WIDTH
        mine = jnp.where((row_id < row_dim) & (col_id < col_dim), mine, 0.0)
        rounded = mine.astype(BF16)
        unit[k, bond] = rounded
        matvec_o[:, cols(k)] = rounded
        for d in (2, 1, 3):
            ag_z(k, d, 0).start()
        square = mine * mine
        return sum(
            square[a : a + 8, b : b + 128] for a in range(0, BLK, 8) for b in range(0, WIDTH, 128)
        )

    def blocks(k, d, first, count):
        return unit.at[k, pl.ds(lax.rem(x + d, 4) * 4 + first, count)]

    def ag_up(k, d):
        return remote(AG_UP + k, blocks(k, d, 0, 4), blocks(k, d, 0, 4), at_x(1))

    def ag_down(k, d):
        return remote(AG_DOWN + k, blocks(k, d, 0, 4), blocks(k, d, 0, 4), at_x(3))

    def fwd_up(k, d):
        return remote(FWD_UP + k, blocks(k, d, 0, 2), blocks(k, d, 0, 2), at_x(1))

    def fwd_down(k, d):
        return remote(FWD_DOWN + k, blocks(k, d, 2, 2), blocks(k, d, 2, 2), at_x(3))

    def gather_z(k):
        for d in (1, 3, 2):
            ag_z(k, d, d).wait_recv()
        ag_up(k, 0).start()
        ag_down(k, 0).start()

    def gather_x(k):
        ag_up(k, 3).wait_recv()
        fwd_up(k, 3).start()
        ag_down(k, 1).wait_recv()
        fwd_down(k, 1).start()

    for p in SECOND:
        pl.when(z == 3)(lambda: rising.leave(p).start())
        pl.when(z == 0)(lambda: falling.leave(p).start())
    for k in chunks:
        sum_over_x(k)

    for p in (3, 4, 0):
        forward(p)

    def spread(i, stage, devices):
        return [
            remote(i + n, part.at[stage], part_in.at[i - SUM_Z + n], device) for n, device in enumerate(devices)
        ]

    sums = [
        spread(SUM_Z, 0, [at_z(1), at_z(2), at_z(3)]),
        spread(SUM_X, 1, [at_x(1), at_x(2), at_x(3)]),
        spread(SUM_S, 2, sectors),
    ]
    starts = [0, 3, 6, 13]

    def sum_start(stage, value):
        part[stage] = value
        for copy in sums[stage]:
            copy.start()

    def sum_finish(stage):
        for copy in sums[stage]:
            copy.wait_recv()
        return sum((part_in[n] for n in range(starts[stage], starts[stage + 1])), part[stage])

    sum_start(0, sum_over_z(0) + sum_over_z(1) + sum_over_z(2))
    for p in SECOND:
        pl.when(z != 3)(lambda: rising.direct(p).start())
        pl.when(z != 0)(lambda: falling.direct(p).start())
    rising.start(PIECES - 1)
    falling.start(PIECES - 1)

    forward(1)
    gather_z(0)
    gather_z(1)
    gather_z(2)
    sum_start(1, sum_finish(0))

    w_gain = [[table_s[index_s[w, k]] for k in range(3)] for w in range(2)]
    low_gain = jnp.where(bond > 0, w_gain[0][0], 0.0)
    high_gain = jnp.where(bond < 15, w_gain[1][2], 0.0)

    def mix(p):
        rows = rows_of(p)
        rising.arrive(p)
        falling.arrive(p)
        here = left[0, rows].astype(F32)
        there = left[1, rows].astype(F32)
        mixed[0, rows] = (low_gain * low[rows].astype(F32) + w_gain[0][1] * here + w_gain[0][2] * there).astype(BF16)
        mixed[1, rows] = (w_gain[1][0] * here + w_gain[1][1] * there + high_gain * high[rows].astype(F32)).astype(BF16)

    gather_x(0)
    forward(2)
    gather_x(1)
    gather_x(2)
    forward(5)
    sum_start(2, sum_finish(1))
    for p in (3, 0, 4, 1, 2):
        mix(p)

    def product(k, first, count):
        rows = pl.ds(first, count)
        for w in range(2):
            result = jnp.dot(mixed[w, rows, :], unit[k].reshape(N, WIDTH), preferred_element_type=F32)
            half[w, rows, cols(k)] = (result * LIFT).astype(BF16)

    for k in chunks:
        fwd_up(k, 2).wait_recv()
        fwd_down(k, 2).wait_recv()
        product(k, 0, N - LAST)
        turned[cols(k)] = unit[k].reshape(N, WIDTH).T
    for w in range(2):
        for k in range(N // TILE):
            rows = slice(k * TILE, (k + 1) * TILE)
            grown_sum[w, rows] = jnp.dot(
                turned[rows, : N - LAST], half[w, : N - LAST, :], preferred_element_type=F32
            )
    square_total = jnp.sum(sum_finish(2))
    scale = lax.rsqrt(jnp.full((1, N), square_total * (1.0 / (8 * N * N)) + 1e-06, F32))
    mix(PIECES - 1)
    for k in chunks:
        product(k, N - LAST, LAST)
    stores = []
    for w in range(2):
        for k in range(N // TILE):
            rows = pl.ds(k * TILE, TILE)
            result = grown_sum[w, rows] + jnp.dot(
                turned[rows, N - LAST :], half[w, N - LAST :, :], preferred_element_type=F32
            )
            grown[w, rows] = (result * scale * (scale * (1.0 / (LIFT * math.sqrt(N))))).astype(BF16)
            stores.append(pltpu.make_async_copy(grown.at[w, rows], env_o.at[w, 0, rows], store_sem.at[3 * w + k]))
            stores[-1].start()

    for k in chunks:
        for copy in (relay_up[k], relay_down[k], up_a[k], up_b[k], down_a[k], down_b[k]):
            copy.wait_send()
        for d in (1, 2, 3):
            rs_z(k, d).wait_send()
            ag_z(k, d, 0).wait_send()
        for copy in (ag_up(k, 0), ag_down(k, 0), fwd_up(k, 3), fwd_down(k, 1)):
            copy.wait_send()
    for stage in sums:
        for copy in stage:
            copy.wait_send()
    for p in range(PIECES):
        rising.sent(p)
        falling.sent(p)
    for store in stores:
        store.wait()


def hand_on(matvec_h, env_h, matvec_o, env_o, matvec, env, load_sem, store_sem):
    loads = [pltpu.make_async_copy(matvec_h, matvec, load_sem.at[0])]
    stores = [pltpu.make_async_copy(matvec, matvec_o, store_sem.at[0])]
    for w in range(2):
        for k in range(N // TILE):
            n = 3 * w + k
            rows = pl.ds(k * TILE, TILE)
            loads.append(pltpu.make_async_copy(env_h.at[w, 0, rows], env.at[n], load_sem.at[n + 1]))
            stores.append(pltpu.make_async_copy(env.at[n], env_o.at[w, 0, rows], store_sem.at[n + 1]))
    for load in loads:
        load.start()
    for load, store in zip(loads, stores):
        load.wait()
        store.start()
    for store in stores:
        store.wait()


def on_device(
    theta, sector_dims, right_dims, env_left, env_right, mpo_on, mpo_coef, mix_index, weight_table
):
    hbm = pl.BlockSpec(memory_space=pl.ANY)
    vmem = pl.BlockSpec(memory_space=pltpu.VMEM)
    matvec, env_next = pl.pallas_call(
        body,
        out_shape=(
            jax.ShapeDtypeStruct((BLK, N), BF16),
            jax.ShapeDtypeStruct(env_left.shape, BF16),
        ),
        in_specs=[hbm] * 9,
        out_specs=(vmem, hbm),
        scratch_shapes=[
            pltpu.SMEM((1,), jnp.int32),
            pltpu.SMEM((1,), jnp.int32),
            pltpu.SMEM((2,), jnp.int32),
            pltpu.SMEM((2,), F32),
            pltpu.SMEM((2, 3), jnp.int32),
            pltpu.SMEM((8,), F32),
            pltpu.VMEM((N, N), BF16),
            pltpu.VMEM((2, N, N), BF16),
            pltpu.VMEM((2, N, N), BF16),
            pltpu.VMEM((N, N), BF16),
            pltpu.VMEM((N, N), BF16),
            pltpu.VMEM((PIECES, max(SIZES), N), BF16),
            pltpu.VMEM((PIECES, max(SIZES), N), BF16),
            pltpu.VMEM((4, 4, BLK, N), F32),
            pltpu.VMEM((2, CHUNKS, 2, BLK, WIDTH), BF16),
            pltpu.VMEM((2, CHUNKS, 2, BLK, WIDTH), BF16),
            pltpu.VMEM((2, CHUNKS, 4, BLK, WIDTH), BF16),
            pltpu.VMEM((CHUNKS, 4, BLK, WIDTH), BF16),
            pltpu.VMEM((CHUNKS, 4, BLK, WIDTH), BF16),
            pltpu.VMEM((CHUNKS, 3, BLK, WIDTH), BF16),
            pltpu.VMEM((CHUNKS, 3, BLK, WIDTH), BF16),
            pltpu.VMEM((CHUNKS, 16, BLK, WIDTH), BF16),
            pltpu.VMEM((N, N), BF16),
            pltpu.VMEM((3, 8, 128), F32),
            pltpu.VMEM((13, 8, 128), F32),
            pltpu.VMEM((2, N, N), BF16),
            pltpu.VMEM((2, N, N), BF16),
            pltpu.VMEM((2, N, N), F32),
            pltpu.VMEM((2, N, N), BF16),
            pltpu.SemaphoreType.DMA((6,)),
            pltpu.SemaphoreType.DMA((5,)),
            pltpu.SemaphoreType.DMA((COPIES,)),
            pltpu.SemaphoreType.DMA((COPIES,)),
            pltpu.SemaphoreType.DMA((6,)),
        ],
        compiler_params=pltpu.CompilerParams(
            collective_id=0, has_side_effects=True, vmem_limit_bytes=56 * 1024 * 1024
        ),
        name="sweep",
    )(theta, env_left, env_right, sector_dims, right_dims, mpo_on, mpo_coef, mix_index, weight_table)
    matvec, env_next = pl.pallas_call(
        hand_on,
        out_shape=(jax.ShapeDtypeStruct((BLK, N), BF16), jax.ShapeDtypeStruct(env_left.shape, BF16)),
        in_specs=[hbm, hbm],
        out_specs=(hbm, hbm),
        scratch_shapes=[
            pltpu.VMEM((BLK, N), BF16),
            pltpu.VMEM((6, TILE, N), BF16),
            pltpu.SemaphoreType.DMA((7,)),
            pltpu.SemaphoreType.DMA((7,)),
        ],
        compiler_params=pltpu.CompilerParams(vmem_limit_bytes=56 * 1024 * 1024),
        name="hand_on",
    )(matvec, env_next)
    return (matvec[None], env_next)


def solution(mesh):
    split = Mesh(mesh.devices.reshape(4, 4, 4, 2), AXES)
    in_specs = (
        P(SECTOR, None, None),
        P(SECTOR),
        P(SECTOR),
        P(BOND, SECTOR, None, None),
        P(BOND, SECTOR, None, None),
        P(BOND),
        P(BOND),
        P(BOND, None),
        P(),
    )
    out_specs = (P(SECTOR, BOND, None), P(BOND, SECTOR, None, None))
    return jax.shard_map(on_device, mesh=split, in_specs=in_specs, out_specs=out_specs, check_vma=False)
```
